32 devices in a mesh: groups: 2 (over y), ctx: 16 (over z, x, core).
Axes of the slice: x: 2, y: 2, z: 4, core: 2. Of those that a mesh axis runs over, the one named last changes fastest.
Arguments:
- query_rows: bfloat16 [4096, 2560], P(('groups', 'ctx')), parts along dimension 0, may hold values from -211 to 211
- key_rows: bfloat16 [4096, 2560], P(('groups', 'ctx')), parts along dimension 0, may hold values from -6.2 to 6.2
- value_rows: bfloat16 [4096, 2560], P(('groups', 'ctx')), parts along dimension 0, may hold values from -6 to 6
- out_grad: bfloat16 [4096, 2560], P(('groups', 'ctx')), parts along dimension 0, may hold values from -6 to 6
- selected: int32 [32, 8], P('groups'), parts along dimension 0, may hold values from 0 to 15, as said below
Outputs:
- attended: bfloat16 [4096, 2560], P(('groups', 'ctx')), parts along dimension 0
- grad_query: bfloat16 [4096, 2560], P(('groups', 'ctx')), parts along dimension 0
- grad_key: bfloat16 [4096, 2560], P(('groups', 'ctx')), parts along dimension 0
- grad_value: bfloat16 [4096, 2560], P(('groups', 'ctx')), parts along dimension 0
- pooled_key_grad: float32 [64, 2560], P(('groups', 'ctx')), parts along dimension 0
- pooled_value_grad: float32 [64, 2560], P(('groups', 'ctx')), parts along dimension 0
The draws below stay inside these ranges and needn't reach their ends.
There are 2 independent parts, one for each index of `groups`. The reference program is written for one: setup_inputs(seed, part) draws one part's arguments, and reference() takes and returns one part's arrays. A program takes and returns all parts, laid end to end along the dimension named above; each array names one. Nothing has to cross between parts.
Inputs may be any that keep to these rules, and one draw needn't show every extreme that they name: `selected`: each row names 8 different tiles.
All inputs are finite; a program needn't handle non-finite values.
Results may differ from the reference program's by a relative error of at most 0.029.
Values may be sent and summed in bfloat16 or wider, within the bound.
No kernel may reach another device: no remote copies, remote signals or barrier semaphores. Data moves between devices by JAX's collectives and lax.ppermute only.
A program may use at most 192 MiB of HBM per device.

```python
import jax
import jax.numpy as jnp
from jax import lax

HEADS = 20
HEAD_DIM = 128
TILE = 128
POOL = 64
SEL = 8
TILES = 16
TOKENS = 2048
COMP = 32


def draw_selected(key, part):
    seeded = jax.random.fold_in(key, 101)
    popular = jax.random.randint(jax.random.fold_in(seeded, 1), (TILES,), 0, 4)
    jitter = jax.random.randint(jax.random.fold_in(seeded, 2), (TILES, TILES), 0, 4096)
    tile_ids = jnp.arange(TILES, dtype=jnp.int32)
    order = jax.random.permutation(jax.random.fold_in(seeded, 3), TILES).astype(jnp.int32)
    place = jnp.zeros((TILES,), jnp.int32).at[order].set(tile_ids)
    offset = (place[None, :] - tile_ids[:, None]) % TILES
    base = (offset < SEL // 2).astype(jnp.int32)
    ranking = (jitter + 1024 * popular[None, :] + 16384 * base) * TILES + tile_ids[None, :]
    return lax.top_k(ranking, SEL)[1].astype(jnp.int32)


def block_rows(key, stamp):
    columns = HEADS * HEAD_DIM
    common = jax.random.normal(jax.random.fold_in(key, stamp), (COMP, 1, columns), jnp.float32)
    jitter = jax.random.normal(jax.random.fold_in(key, stamp + 1), (COMP, POOL, columns), jnp.float32)
    return jnp.clip((common + jitter) * 0.7071, -6.0, 6.0).reshape(TOKENS, columns)


def draw_key_rows(key, part):
    result = block_rows(key, 201)
    return jnp.clip(result, -6.2, 6.2).astype(jnp.bfloat16)


def draw_query_rows(key, part):
    columns = HEADS * HEAD_DIM
    result = jnp.clip(1.5 * jax.random.normal(jax.random.fold_in(key, 401), (TOKENS, columns), jnp.float32), -8.0, 8.0)
    return result.astype(jnp.bfloat16)


def draw_value_rows(key, part):
    return block_rows(key, 301).astype(jnp.bfloat16)


def draw_out_grad(key, part):
    columns = HEADS * HEAD_DIM
    result = jax.random.normal(jax.random.fold_in(key, 502), (TOKENS, columns), jnp.float32)
    return jnp.clip(result, -6.0, 6.0).astype(jnp.bfloat16)


def setup_inputs(seed: int = 0, part: int = 0) -> dict:
    key_list = jax.random.split(jax.random.key(seed), 6)
    part_splits = jax.random.split(jax.random.fold_in(key_list[5], part), 6)
    return {
        "query_rows": draw_query_rows(jax.random.fold_in(jax.random.fold_in(key_list[5], part), 71), part),
        "key_rows": draw_key_rows(jax.random.fold_in(jax.random.fold_in(key_list[5], part), 71), part),
        "value_rows": draw_value_rows(jax.random.fold_in(jax.random.fold_in(key_list[5], part), 71), part),
        "out_grad": draw_out_grad(jax.random.fold_in(jax.random.fold_in(key_list[5], part), 71), part),
        "selected": draw_selected(jax.random.fold_in(jax.random.fold_in(key_list[5], part), 71), part),
    }


def pooled(rows):
    return jnp.mean(rows.astype(jnp.float32).reshape(-1, POOL, rows.shape[1]), axis=1).astype(jnp.bfloat16)


def settle(array):
    return lax.optimization_barrier(array.astype(jnp.bfloat16)).astype(jnp.float32)


def tile_pass(queries, grads_out, keys_all, values_all):
    scaling = HEAD_DIM ** -0.5
    height = queries.shape[0]
    key_count = keys_all.shape[0]
    columns = HEADS * HEAD_DIM
    highest = lax.Precision.HIGHEST
    head_query = queries.astype(jnp.float32).reshape(height, HEADS, HEAD_DIM)
    head_grad = grads_out.astype(jnp.float32).reshape(height, HEADS, HEAD_DIM)
    head_key = keys_all.astype(jnp.float32).reshape(key_count, HEADS, HEAD_DIM)
    head_value = values_all.astype(jnp.float32).reshape(key_count, HEADS, HEAD_DIM)
    scores = jnp.einsum("rhd,khd->hrk", head_query, head_key, precision=highest) * scaling
    summit = jnp.max(scores, axis=-1, keepdims=True)
    raised = jnp.exp(scores - summit)
    weights = raised / jnp.sum(raised, axis=-1, keepdims=True)
    rounded = settle(weights)
    attended = jnp.einsum("hrk,khd->rhd", rounded, head_value, precision=highest).astype(jnp.bfloat16)
    row_dots = jnp.sum(head_grad * attended.astype(jnp.float32), axis=-1)
    prob_grad = jnp.einsum("rhd,khd->hrk", head_grad, head_value, precision=highest)
    score_grad = settle(weights * (prob_grad - row_dots.T[:, :, None]))
    grad_query = (jnp.einsum("hrk,khd->rhd", score_grad, head_key, precision=highest) * scaling).astype(jnp.bfloat16)
    key_terms = jnp.einsum("hrk,rhd->khd", score_grad, head_query, precision=highest) * scaling
    value_terms = jnp.einsum("hrk,rhd->khd", rounded, head_grad, precision=highest)
    return (attended.reshape(height, columns), grad_query.reshape(height, columns),
            key_terms.reshape(key_count, columns), value_terms.reshape(key_count, columns))


def reference(query_rows, key_rows, value_rows, out_grad, selected):
    columns = HEADS * HEAD_DIM
    pool_keys = pooled(key_rows)
    pool_values = pooled(value_rows)
    key_tiles = key_rows.reshape(TILES, TILE, columns)
    value_tiles = value_rows.reshape(TILES, TILE, columns)

    def advance(totals, inputs):
        coarse_keys, coarse_values, fine_keys, fine_values = totals
        queries, grads_out, listed = inputs
        keys_all = jnp.concatenate([pool_keys, key_tiles[listed].reshape(SEL * TILE, columns)], axis=0)
        values_all = jnp.concatenate([pool_values, value_tiles[listed].reshape(SEL * TILE, columns)], axis=0)
        attended, grad_query, key_terms, value_terms = tile_pass(queries, grads_out, keys_all, values_all)
        coarse_keys = coarse_keys + key_terms[:COMP]
        coarse_values = coarse_values + value_terms[:COMP]
        fine_keys = fine_keys.at[listed].add(settle(key_terms[COMP:]).reshape(SEL, TILE, columns))
        fine_values = fine_values.at[listed].add(settle(value_terms[COMP:]).reshape(SEL, TILE, columns))
        return (coarse_keys, coarse_values, fine_keys, fine_values), (attended, grad_query)

    initial = (jnp.zeros((COMP, columns), jnp.float32), jnp.zeros((COMP, columns), jnp.float32),
               jnp.zeros((TILES, TILE, columns), jnp.float32), jnp.zeros((TILES, TILE, columns), jnp.float32))
    totals, outputs = lax.scan(advance, initial, (query_rows.reshape(TILES, TILE, columns),
                                                  out_grad.reshape(TILES, TILE, columns), selected))
    coarse_keys, coarse_values, fine_keys, fine_values = totals
    attended = outputs[0].reshape(TOKENS, columns)
    grad_query = outputs[1].reshape(TOKENS, columns)
    grad_key = (settle(fine_keys.reshape(TOKENS, columns)) + jnp.repeat(coarse_keys, POOL, axis=0) / POOL).astype(jnp.bfloat16)
    grad_value = (settle(fine_values.reshape(TOKENS, columns)) + jnp.repeat(coarse_values, POOL, axis=0) / POOL).astype(jnp.bfloat16)
    return (attended, grad_query, grad_key, grad_value, coarse_keys, coarse_values)
```

```python
import functools

import jax
import jax.numpy as jnp
from jax import lax
from jax.experimental import pallas as pl
from jax.experimental.pallas import tpu as pltpu
from jax.sharding import PartitionSpec as P

HEADS = 20
HEAD_DIM = 128
TILE = 128
POOL = 64
SEL = 8


def pooled(rows):
    return jnp.mean(rows.astype(jnp.float32).reshape(-1, POOL, rows.shape[1]), axis=1).astype(
        jnp.bfloat16
    )


def contract(left, right, left_dim, right_dim):
    return lax.dot_general(
        left, right, (((left_dim,), (right_dim,)), ((), ())), preferred_element_type=jnp.float32
    )


def attend(queries, grads_out, keys_all, values_all):
    scaling = HEAD_DIM ** (-0.5)
    out_parts, query_parts, key_parts, value_parts = ([], [], [], [])
    for head in range(HEADS):
        lower = head * HEAD_DIM
        upper = lower + HEAD_DIM
        head_query = queries[:, lower:upper]
        head_grad = grads_out[:, lower:upper]
        head_key = keys_all[:, lower:upper]
        head_value = values_all[:, lower:upper]
        scores = contract(head_query, head_key, 1, 1) * scaling
        summit = jnp.max(scores, axis=-1, keepdims=True)
        raised = jnp.exp(scores - summit)
        weights = raised / jnp.sum(raised, axis=-1, keepdims=True)
        rounded = weights.astype(jnp.bfloat16)
        out_rows = jnp.dot(rounded, head_value, preferred_element_type=jnp.float32).astype(
            jnp.bfloat16
        )
        row_dots = jnp.sum(
            head_grad.astype(jnp.float32) * out_rows.astype(jnp.float32), axis=-1, keepdims=True
        )
        prob_grad = contract(head_grad, head_value, 1, 1)
        score_grad = (weights * (prob_grad - row_dots)).astype(jnp.bfloat16)
        query_grad = jnp.dot(score_grad, head_key, preferred_element_type=jnp.float32) * scaling
        key_terms = contract(score_grad, head_query, 0, 0) * scaling
        value_terms = contract(rounded, head_grad, 0, 0)
        out_parts.append(out_rows)
        query_parts.append(query_grad.astype(jnp.bfloat16))
        key_parts.append(key_terms)
        value_parts.append(value_terms)
    return (
        jnp.concatenate(out_parts, axis=1),
        jnp.concatenate(query_parts, axis=1),
        jnp.concatenate(key_parts, axis=1),
        jnp.concatenate(value_parts, axis=1),
    )


def package(tiles_in, pooled_in, devices, spread):
    tiles_here, tile_len, columns = tiles_in.shape
    per_tile = tile_len // POOL
    split_rows = tiles_in.reshape(tiles_here, devices, spread, columns)
    copies = jnp.broadcast_to(
        pooled_in.reshape(tiles_here, 1, per_tile, columns),
        (tiles_here, devices, per_tile, columns),
    )
    return jnp.concatenate([split_rows, copies], axis=2).reshape(
        tiles_here, devices * (spread + per_tile), columns
    )


def listed_shards(query_rows, key_rows, value_rows, out_grad, selected):
    height, columns = query_rows.shape
    devices = lax.axis_size("ctx")
    tiles_here = height // TILE
    spread = TILE // devices
    own_keys = pooled(key_rows)
    own_values = pooled(value_rows)
    key_tiles = key_rows.reshape(tiles_here, TILE, columns)
    value_tiles = value_rows.reshape(tiles_here, TILE, columns)
    joined_keys, joined_values = (
        lax.all_to_all(
            package(key_tiles, own_keys, devices, spread),
            "ctx",
            split_axis=1,
            concat_axis=0,
            tiled=True,
        ),
        lax.all_to_all(
            package(value_tiles, own_values, devices, spread),
            "ctx",
            split_axis=1,
            concat_axis=0,
            tiled=True,
        ),
    )
    held_keys = joined_keys[:, :spread]
    held_values = joined_values[:, :spread]
    pool_keys = joined_keys[:, spread:].reshape(-1, columns)
    pool_values = joined_values[:, spread:].reshape(-1, columns)
    comp_count = pool_keys.shape[0]
    got_keys, got_values = (
        lax.all_to_all(held_keys[selected], "ctx", split_axis=0, concat_axis=2, tiled=True),
        lax.all_to_all(held_values[selected], "ctx", split_axis=0, concat_axis=2, tiled=True),
    )
    fine_keys = got_keys.reshape(tiles_here, SEL * TILE, columns)
    fine_values = got_values.reshape(tiles_here, SEL * TILE, columns)
    out_tiles, query_tiles, key_listed, value_listed = ([], [], [], [])
    keys_all = jnp.concatenate([pool_keys, fine_keys[0]], axis=0)
    values_all = jnp.concatenate([pool_values, fine_values[0]], axis=0)
    out_rows, query_grad, key_terms, value_terms = attend(
        query_rows, out_grad, keys_all, values_all
    )
    out_tiles.append(out_rows)
    query_tiles.append(query_grad)
    coarse_keys = key_terms[:comp_count]
    coarse_values = value_terms[:comp_count]
    key_listed.append(key_terms[comp_count:].astype(jnp.bfloat16))
    value_listed.append(value_terms[comp_count:].astype(jnp.bfloat16))
    own_coarse_keys, own_coarse_values = (
        lax.psum_scatter(coarse_keys, "ctx", scatter_dimension=0, tiled=True),
        lax.psum_scatter(coarse_values, "ctx", scatter_dimension=0, tiled=True),
    )
    listed_keys = jnp.stack(key_listed).reshape(tiles_here * SEL, devices, spread, columns)
    listed_values = jnp.stack(value_listed).reshape(tiles_here * SEL, devices, spread, columns)
    back_keys, back_values = (
        lax.all_to_all(listed_keys, "ctx", split_axis=1, concat_axis=0, tiled=True),
        lax.all_to_all(listed_values, "ctx", split_axis=1, concat_axis=0, tiled=True),
    )
    tile_ids = jnp.arange(selected.shape[0], dtype=jnp.int32)[:, None]
    member = (selected.reshape(1, -1) == tile_ids).astype(jnp.bfloat16)
    entries = member.shape[1]
    sum_keys = jnp.dot(
        member, back_keys.reshape(entries, spread * columns), preferred_element_type=jnp.float32
    )
    sum_values = jnp.dot(
        member, back_values.reshape(entries, spread * columns), preferred_element_type=jnp.float32
    )
    held_key_grad = sum_keys.astype(jnp.bfloat16).reshape(devices, tiles_here, spread, columns)
    held_value_grad = sum_values.astype(jnp.bfloat16).reshape(devices, tiles_here, spread, columns)
    owned_keys, owned_values = (
        lax.all_to_all(held_key_grad, "ctx", split_axis=0, concat_axis=2, tiled=True),
        lax.all_to_all(held_value_grad, "ctx", split_axis=0, concat_axis=2, tiled=True),
    )
    grad_key = (
        owned_keys.reshape(height, columns).astype(jnp.float32)
        + jnp.repeat(own_coarse_keys, POOL, axis=0) / POOL
    ).astype(jnp.bfloat16)
    grad_value = (
        owned_values.reshape(height, columns).astype(jnp.float32)
        + jnp.repeat(own_coarse_values, POOL, axis=0) / POOL
    ).astype(jnp.bfloat16)
    attended = out_tiles[0]
    grad_query = query_tiles[0]
    return (attended, grad_query, grad_key, grad_value, own_coarse_keys, own_coarse_values)


LANES = 128
SPLITS = 3
VMEM = pl.BlockSpec(memory_space=pltpu.VMEM)
SMEM = pl.BlockSpec(memory_space=pltpu.SMEM)
BIG = pltpu.CompilerParams(vmem_limit_bytes=50 * 1024 * 1024)


def nt(left, right):
    return contract(left, right, 1, 1)


def nn(left, right):
    return contract(left, right, 1, 0)


def split_rows(total):
    parts = []
    for _ in range(SPLITS):
        part = total.astype(jnp.bfloat16)
        parts.append(part.astype(jnp.float32))
        total = total - parts[-1]
    return parts


def tail_rows(coarse_key, coarse_value):
    per_tile = TILE // POOL
    parts = split_rows(jnp.concatenate([coarse_key, coarse_value], axis=0))
    used = SPLITS * 2 * per_tile
    filler = jnp.zeros((tail_height() - used, LANES), jnp.float32)
    return jnp.concatenate(parts + [filler], axis=0).astype(jnp.bfloat16)


def tail_height():
    used = SPLITS * 2 * (TILE // POOL)
    return -(-used // 16) * 16


def join_tail(tail):
    pair = 2 * (TILE // POOL)
    rows = tail.astype(jnp.float32)
    total = rows[:pair]
    for part in range(1, SPLITS):
        total = total + rows[part * pair : (part + 1) * pair]
    return total


def pack_body(q_ref, k_ref, v_ref, g_ref, out_ref):
    for place in range(out_ref.shape[0]):
        columns = slice(place * LANES, (place + 1) * LANES)
        for index, ref in enumerate((q_ref, k_ref, v_ref, g_ref)):
            out_ref[place, index * TILE : (index + 1) * TILE, :] = ref[:, columns]


def pack(arrays, first, count, step):
    spec = pl.BlockSpec((TILE, step * LANES), lambda i: (0, first // step + i))
    return pl.pallas_call(
        pack_body,
        grid=(count // step,),
        in_specs=[spec] * 4,
        out_specs=pl.BlockSpec((step, 4 * TILE, LANES), lambda i: (i, 0, 0)),
        out_shape=jax.ShapeDtypeStruct((count, 4 * TILE, LANES), jnp.bfloat16),
        name="pack",
    )(*arrays)


def prepare(tiles, get_key, get_value, scratch):
    pool_key, pool_value, key_t, value_t, key_sum, value_sum = scratch
    per_tile = TILE // POOL

    def one(tile, carry):
        for get, pool_ref, flip_ref in (
            (get_key, pool_key, key_t),
            (get_value, pool_value, value_t),
        ):
            rows = get(tile).astype(jnp.float32)
            means = [
                jnp.mean(rows[part * POOL : (part + 1) * POOL], axis=0, keepdims=True)
                for part in range(per_tile)
            ]
            pool_ref[pl.ds(tile * per_tile, per_tile), :] = jnp.concatenate(means, axis=0)
            flip_ref[tile] = rows.T.astype(jnp.bfloat16)
        key_sum[tile] = jnp.zeros((TILE, LANES), jnp.float32)
        value_sum[tile] = jnp.zeros((TILE, LANES), jnp.float32)
        return carry

    lax.fori_loop(0, tiles, one, 0)


def one_tile(query, grad, listed, get_key, get_value, scratch, work):
    pool_key, pool_value, key_t, value_t, key_sum, value_sum, pool_key_sum, pool_value_sum = scratch
    score_ref, round_ref, slope_ref = work
    scaling = HEAD_DIM ** (-0.5)
    base2 = scaling * 1.4426950408889634
    comp = pool_key.shape[0]
    coarse_key = pool_key[...].astype(jnp.bfloat16)
    coarse_value = pool_value[...].astype(jnp.bfloat16)
    spans = [(slot * TILE, TILE) for slot in range(SEL)] + [(SEL * TILE, comp)]
    keys = [get_key(tile) for tile in listed] + [coarse_key]
    top = None
    for (start, size), key in zip(spans, keys):
        score = nt(key, query)
        score_ref[start : start + size, :] = score
        peak = jnp.max(score, axis=0, keepdims=True)
        top = peak if top is None else jnp.maximum(top, peak)
    total = jnp.zeros((1, LANES), jnp.float32)
    for start, size in spans:
        raised = jnp.exp2((score_ref[start : start + size, :] - top) * base2)
        score_ref[start : start + size, :] = raised
        total = total + jnp.sum(raised, axis=0, keepdims=True)
    inverse = 1.0 / total
    for start, size in spans:
        weight = score_ref[start : start + size, :] * inverse
        score_ref[start : start + size, :] = weight
        round_ref[start : start + size, :] = weight.astype(jnp.bfloat16)
    values_t = jnp.concatenate([value_t[tile] for tile in listed], axis=1)
    out_t = nn(values_t, round_ref[: SEL * TILE, :]) + contract(
        coarse_value, round_ref[SEL * TILE :, :], 0, 0
    )
    out_t = out_t.astype(jnp.bfloat16).astype(jnp.float32)
    grad_t = grad.astype(jnp.float32).T
    dots = jnp.sum(out_t * grad_t, axis=0, keepdims=True)
    values = [get_value(tile) for tile in listed] + [coarse_value]
    for place, ((start, size), value) in enumerate(zip(spans, values)):
        slope = (score_ref[start : start + size, :] * (nt(value, grad) - dots)).astype(jnp.bfloat16)
        slope_ref[start : start + size, :] = slope
        key_term = nn(slope, query)
        value_term = nn(round_ref[start : start + size, :], grad)
        if place < SEL:
            key_sum[listed[place]] += key_term
            value_sum[listed[place]] += value_term
        else:
            pool_key_sum[...] += key_term
            pool_value_sum[...] += value_term
    keys_t = jnp.concatenate([key_t[tile] for tile in listed], axis=1)
    query_t = nn(keys_t, slope_ref[: SEL * TILE, :]) + contract(
        coarse_key, slope_ref[SEL * TILE :, :], 0, 0
    )
    return out_t.T.astype(jnp.bfloat16), (query_t.T * scaling).astype(jnp.bfloat16)


def finish(tile, scratch):
    scaling = HEAD_DIM ** (-0.5)
    key_sum, value_sum, pool_key_sum, pool_value_sum = scratch
    per_tile = TILE // POOL
    coarse_key = pool_key_sum[pl.ds(tile * per_tile, per_tile), :] * scaling
    coarse_value = pool_value_sum[pl.ds(tile * per_tile, per_tile), :]

    def whole(fine, coarse):
        return jnp.concatenate(
            [
                fine[part * POOL : (part + 1) * POOL] + coarse[part : part + 1] * (1.0 / POOL)
                for part in range(per_tile)
            ],
            axis=0,
        )

    return (
        whole(key_sum[tile] * scaling, coarse_key),
        whole(value_sum[tile], coarse_value),
        coarse_key,
        coarse_value,
    )


def head_scratch(tiles):
    comp = tiles * (TILE // POOL)
    return [
        pltpu.VMEM((comp, LANES), jnp.float32),
        pltpu.VMEM((comp, LANES), jnp.float32),
        pltpu.VMEM((tiles, LANES, TILE), jnp.bfloat16),
        pltpu.VMEM((tiles, LANES, TILE), jnp.bfloat16),
        pltpu.VMEM((tiles, TILE, LANES), jnp.float32),
        pltpu.VMEM((tiles, TILE, LANES), jnp.float32),
        pltpu.VMEM((comp, LANES), jnp.float32),
        pltpu.VMEM((comp, LANES), jnp.float32),
        pltpu.VMEM((SEL * TILE + comp, LANES), jnp.float32),
        pltpu.VMEM((SEL * TILE + comp, LANES), jnp.bfloat16),
        pltpu.VMEM((SEL * TILE + comp, LANES), jnp.bfloat16),
    ]


def whole_head(sel_ref, in_ref, out_ref, *scratch):
    tiles = in_ref.shape[0]
    totals, work = scratch[:8], scratch[8:]

    def get_key(tile):
        return in_ref[tile, TILE : 2 * TILE, :]

    def get_value(tile):
        return in_ref[tile, 2 * TILE : 3 * TILE, :]

    prepare(tiles, get_key, get_value, totals[:6])
    totals[6][...] = jnp.zeros_like(totals[6])
    totals[7][...] = jnp.zeros_like(totals[7])

    def one(tile, carry):
        listed = [sel_ref[tile, slot] for slot in range(SEL)]
        rows, slopes = one_tile(
            in_ref[tile, :TILE, :],
            in_ref[tile, 3 * TILE :, :],
            listed,
            get_key,
            get_value,
            totals,
            work,
        )
        out_ref[tile, :TILE, :] = rows
        out_ref[tile, TILE : 2 * TILE, :] = slopes
        return carry

    lax.fori_loop(0, tiles, one, 0)

    def last(tile, carry):
        key, value, coarse_key, coarse_value = finish(tile, totals[4:])
        out_ref[tile, 2 * TILE : 3 * TILE, :] = key.astype(jnp.bfloat16)
        out_ref[tile, 3 * TILE : 4 * TILE, :] = value.astype(jnp.bfloat16)
        out_ref[tile, 4 * TILE :, :] = tail_rows(coarse_key, coarse_value)
        return carry

    lax.fori_loop(0, tiles, last, 0)


def shared_head(span, planes, place_ref, sel_ref, own_ref, *refs):
    pieces = refs[: span - 1]
    out_ref, keep_ref = refs[span - 1 : span + 1]
    send_refs = refs[span + 1 : 2 * span]
    keys, values = refs[2 * span : 2 * span + 2]
    scratch = refs[2 * span + 2 :]
    totals, work = scratch[:8], scratch[8:]
    tiles = span * planes
    place = place_ref[0]
    for step in range(span):
        for plane in range(planes):
            tile = plane * span + lax.bitwise_xor(place, step)
            if step == 0:
                keys[tile] = own_ref[plane, TILE : 2 * TILE, :]
                values[tile] = own_ref[plane, 2 * TILE : 3 * TILE, :]
            else:
                keys[tile] = pieces[step - 1][plane, :TILE, :]
                values[tile] = pieces[step - 1][plane, TILE:, :]

    def get_key(tile):
        return keys[tile]

    def get_value(tile):
        return values[tile]

    prepare(tiles, get_key, get_value, totals[:6])
    totals[6][...] = jnp.zeros_like(totals[6])
    totals[7][...] = jnp.zeros_like(totals[7])

    def one(plane, carry):
        listed = [sel_ref[plane * span + place, slot] for slot in range(SEL)]
        rows, slopes = one_tile(
            own_ref[plane, :TILE, :],
            own_ref[plane, 3 * TILE :, :],
            listed,
            get_key,
            get_value,
            totals,
            work,
        )
        out_ref[plane, :TILE, :] = rows
        out_ref[plane, TILE:, :] = slopes
        return carry

    lax.fori_loop(0, planes, one, 0)
    for step in range(span):
        def last(plane, carry, step=step):
            tile = plane * span + lax.bitwise_xor(place, step)
            key, value, coarse_key, coarse_value = finish(tile, totals[4:])
            if step == 0:
                pair = 2 * (TILE // POOL)
                keep_ref[plane, :TILE, :] = key
                keep_ref[plane, TILE : 2 * TILE, :] = value
                keep_ref[plane, 2 * TILE : 2 * TILE + 8, :] = jnp.concatenate(
                    [coarse_key, coarse_value, jnp.zeros((8 - pair, LANES), jnp.float32)], axis=0
                )
            else:
                ref = send_refs[step - 1]
                ref[plane, :TILE, :] = key.astype(jnp.bfloat16)
                ref[plane, TILE : 2 * TILE, :] = value.astype(jnp.bfloat16)
                ref[plane, 2 * TILE :, :] = tail_rows(coarse_key, coarse_value)
            return carry

        lax.fori_loop(0, planes, last, 0)


def gather_terms(span, rows_ref, keep_ref, *refs):
    pieces, out_ref = refs[: span - 1], refs[span - 1]
    per_tile = TILE // POOL

    def one(plane, carry):
        fine = keep_ref[plane, : 2 * TILE, :]
        coarse = keep_ref[plane, 2 * TILE : 2 * TILE + 2 * per_tile, :]
        for piece in pieces:
            fine = fine + piece[plane, : 2 * TILE, :].astype(jnp.float32)
            coarse = coarse + join_tail(piece[plane, 2 * TILE :, :])
        out_ref[plane, : 2 * TILE, :] = rows_ref[plane]
        out_ref[plane, 2 * TILE : 4 * TILE, :] = fine.astype(jnp.bfloat16)
        out_ref[plane, 4 * TILE :, :] = tail_rows(coarse[:per_tile], coarse[per_tile:])
        return carry

    lax.fori_loop(0, rows_ref.shape[0], one, 0)


def unpack_body(main_ref, rest_ref, a_ref, q_ref, k_ref, v_ref, pk_ref, pv_ref):
    per_tile = TILE // POOL
    heads = main_ref.shape[0]
    for head in range(heads + rest_ref.shape[0]):
        ref, place = (main_ref, head) if head < heads else (rest_ref, head - heads)
        columns = slice(head * LANES, (head + 1) * LANES)
        for index, out in enumerate((a_ref, q_ref, k_ref, v_ref)):
            out[:, columns] = ref[place, index * TILE : (index + 1) * TILE, :]
        coarse = join_tail(ref[place, 4 * TILE :, :])
        pk_ref[:, columns] = coarse[:per_tile]
        pv_ref[:, columns] = coarse[per_tile:]


def head_shards(query_rows, key_rows, value_rows, out_grad, selected):
    devices = lax.axis_size("ctx")
    height, columns = query_rows.shape
    planes = HEADS - devices
    span = devices // planes
    arrays = (query_rows, key_rows, value_rows, out_grad)
    place = jnp.reshape(lax.axis_index("ctx") % span, (1,))
    columns_of = [[p * span + w for p in range(planes)] for w in range(span)]

    def shift(block, step):
        return lax.ppermute(block, "ctx", [(i, i ^ step) for i in range(devices)])

    def swap(block, groups=None):
        return lax.all_to_all(block, "ctx", 0, 0, axis_index_groups=groups, tiled=True)

    block = 4 * TILE + tail_height()
    part = 2 * TILE + tail_height()
    own = swap(pack(arrays, devices, planes, planes), columns_of)
    main = swap(pack(arrays, 0, devices, 4))
    own_kv = own[:, TILE : 3 * TILE, :]
    pieces = [shift(own_kv, step) for step in range(1, span)]
    outs = pl.pallas_call(
        functools.partial(shared_head, span, planes),
        in_specs=[SMEM, SMEM] + [VMEM] * span,
        out_specs=[VMEM] * (span + 1),
        out_shape=[
            jax.ShapeDtypeStruct((planes, 2 * TILE, LANES), jnp.bfloat16),
            jax.ShapeDtypeStruct((planes, 2 * TILE + 8, LANES), jnp.float32),
        ]
        + [jax.ShapeDtypeStruct((planes, part, LANES), jnp.bfloat16)] * (span - 1),
        scratch_shapes=[pltpu.VMEM((devices, TILE, LANES), jnp.bfloat16)] * 2
        + head_scratch(devices),
        compiler_params=BIG,
        name="shared_head",
    )(place, selected, own, *pieces)
    terms = [shift(sent, step + 1) for step, sent in enumerate(outs[2:])]
    rest = pl.pallas_call(
        functools.partial(gather_terms, span),
        in_specs=[VMEM] * (span + 1),
        out_specs=VMEM,
        out_shape=jax.ShapeDtypeStruct((planes, block, LANES), jnp.bfloat16),
        compiler_params=BIG,
        name="gather_terms",
    )(outs[0], outs[1], *terms)
    rest = swap(rest, columns_of)
    done = pl.pallas_call(
        whole_head,
        in_specs=[SMEM, VMEM],
        out_specs=VMEM,
        out_shape=jax.ShapeDtypeStruct((devices, block, LANES), jnp.bfloat16),
        scratch_shapes=head_scratch(devices),
        compiler_params=BIG,
        name="whole_head",
    )(selected, main)
    done = swap(done)
    wide = jax.ShapeDtypeStruct((height, columns), jnp.bfloat16)
    thin = jax.ShapeDtypeStruct((height // POOL, columns), jnp.float32)
    return pl.pallas_call(
        unpack_body,
        in_specs=[VMEM, VMEM],
        out_specs=[VMEM] * 6,
        out_shape=[wide, wide, wide, wide, thin, thin],
        compiler_params=BIG,
        name="unpack",
    )(done, rest)


def shards(query_rows, key_rows, value_rows, out_grad, selected):
    devices = lax.axis_size("ctx")
    planes = HEADS - devices
    tiles_here = query_rows.shape[0] // TILE
    if planes > 0 and devices % planes == 0 and tiles_here == 1:
        span = devices // planes
        if span & (span - 1) == 0:
            return head_shards(query_rows, key_rows, value_rows, out_grad, selected)
    return listed_shards(query_rows, key_rows, value_rows, out_grad, selected)


def solution(mesh):
    in_specs = (
        P(("groups", "ctx"), None),
        P(("groups", "ctx"), None),
        P(("groups", "ctx"), None),
        P(("groups", "ctx"), None),
        P("groups", None),
    )
    out_specs = (
        P(("groups", "ctx"), None),
        P(("groups", "ctx"), None),
        P(("groups", "ctx"), None),
        P(("groups", "ctx"), None),
        P(("groups", "ctx"), None),
        P(("groups", "ctx"), None),
    )
    return jax.shard_map(shards, mesh=mesh, in_specs=in_specs, out_specs=out_specs, check_vma=False)
```

```python
import functools

import jax
import jax.numpy as jnp
from jax import lax
from jax.experimental import pallas as pl
from jax.experimental.pallas import tpu as pltpu
from jax.sharding import PartitionSpec as P


HEADS = 20
HEAD_DIM = 128
TILE = 128
POOL = 64
SEL = 8


def pooled(rows):
    return jnp.mean(rows.astype(jnp.float32).reshape(-1, POOL, rows.shape[1]), axis=1).astype(
        jnp.bfloat16
    )


def contract(left, right, left_dim, right_dim):
    return lax.dot_general(
        left, right, (((left_dim,), (right_dim,)), ((), ())), preferred_element_type=jnp.float32
    )


def attend(queries, grads_out, keys_all, values_all):
    scaling = HEAD_DIM ** (-0.5)
    out_parts, query_parts, key_parts, value_parts = ([], [], [], [])
    for head in range(HEADS):
        lower = head * HEAD_DIM
        upper = lower + HEAD_DIM
        head_query = queries[:, lower:upper]
        head_grad = grads_out[:, lower:upper]
        head_key = keys_all[:, lower:upper]
        head_value = values_all[:, lower:upper]
        scores = contract(head_query, head_key, 1, 1) * scaling
        summit = jnp.max(scores, axis=-1, keepdims=True)
        raised = jnp.exp(scores - summit)
        weights = raised / jnp.sum(raised, axis=-1, keepdims=True)
        rounded = weights.astype(jnp.bfloat16)
        out_rows = jnp.dot(rounded, head_value, preferred_element_type=jnp.float32).astype(
            jnp.bfloat16
        )
        row_dots = jnp.sum(
            head_grad.astype(jnp.float32) * out_rows.astype(jnp.float32), axis=-1, keepdims=True
        )
        prob_grad = contract(head_grad, head_value, 1, 1)
        score_grad = (weights * (prob_grad - row_dots)).astype(jnp.bfloat16)
        query_grad = jnp.dot(score_grad, head_key, preferred_element_type=jnp.float32) * scaling
        key_terms = contract(score_grad, head_query, 0, 0) * scaling
        value_terms = contract(rounded, head_grad, 0, 0)
        out_parts.append(out_rows)
        query_parts.append(query_grad.astype(jnp.bfloat16))
        key_parts.append(key_terms)
        value_parts.append(value_terms)
    return (
        jnp.concatenate(out_parts, axis=1),
        jnp.concatenate(query_parts, axis=1),
        jnp.concatenate(key_parts, axis=1),
        jnp.concatenate(value_parts, axis=1),
    )


def package(tiles_in, pooled_in, devices, spread):
    tiles_here, tile_len, columns = tiles_in.shape
    per_tile = tile_len // POOL
    split_rows = tiles_in.reshape(tiles_here, devices, spread, columns)
    copies = jnp.broadcast_to(
        pooled_in.reshape(tiles_here, 1, per_tile, columns),
        (tiles_here, devices, per_tile, columns),
    )
    return jnp.concatenate([split_rows, copies], axis=2).reshape(
        tiles_here, devices * (spread + per_tile), columns
    )


def listed_shards(query_rows, key_rows, value_rows, out_grad, selected):
    height, columns = query_rows.shape
    devices = lax.axis_size("ctx")
    tiles_here = height // TILE
    spread = TILE // devices
    own_keys = pooled(key_rows)
    own_values = pooled(value_rows)
    key_tiles = key_rows.reshape(tiles_here, TILE, columns)
    value_tiles = value_rows.reshape(tiles_here, TILE, columns)
    joined_keys, joined_values = (
        lax.all_to_all(
            package(key_tiles, own_keys, devices, spread),
            "ctx",
            split_axis=1,
            concat_axis=0,
            tiled=True,
        ),
        lax.all_to_all(
            package(value_tiles, own_values, devices, spread),
            "ctx",
            split_axis=1,
            concat_axis=0,
            tiled=True,
        ),
    )
    held_keys = joined_keys[:, :spread]
    held_values = joined_values[:, :spread]
    pool_keys = joined_keys[:, spread:].reshape(-1, columns)
    pool_values = joined_values[:, spread:].reshape(-1, columns)
    comp_count = pool_keys.shape[0]
    got_keys, got_values = (
        lax.all_to_all(held_keys[selected], "ctx", split_axis=0, concat_axis=2, tiled=True),
        lax.all_to_all(held_values[selected], "ctx", split_axis=0, concat_axis=2, tiled=True),
    )
    fine_keys = got_keys.reshape(tiles_here, SEL * TILE, columns)
    fine_values = got_values.reshape(tiles_here, SEL * TILE, columns)
    out_tiles, query_tiles, key_listed, value_listed = ([], [], [], [])
    keys_all = jnp.concatenate([pool_keys, fine_keys[0]], axis=0)
    values_all = jnp.concatenate([pool_values, fine_values[0]], axis=0)
    out_rows, query_grad, key_terms, value_terms = attend(
        query_rows, out_grad, keys_all, values_all
    )
    out_tiles.append(out_rows)
    query_tiles.append(query_grad)
    coarse_keys = key_terms[:comp_count]
    coarse_values = value_terms[:comp_count]
    key_listed.append(key_terms[comp_count:].astype(jnp.bfloat16))
    value_listed.append(value_terms[comp_count:].astype(jnp.bfloat16))
    own_coarse_keys, own_coarse_values = (
        lax.psum_scatter(coarse_keys, "ctx", scatter_dimension=0, tiled=True),
        lax.psum_scatter(coarse_values, "ctx", scatter_dimension=0, tiled=True),
    )
    listed_keys = jnp.stack(key_listed).reshape(tiles_here * SEL, devices, spread, columns)
    listed_values = jnp.stack(value_listed).reshape(tiles_here * SEL, devices, spread, columns)
    back_keys, back_values = (
        lax.all_to_all(listed_keys, "ctx", split_axis=1, concat_axis=0, tiled=True),
        lax.all_to_all(listed_values, "ctx", split_axis=1, concat_axis=0, tiled=True),
    )
    tile_ids = jnp.arange(selected.shape[0], dtype=jnp.int32)[:, None]
    member = (selected.reshape(1, -1) == tile_ids).astype(jnp.bfloat16)
    entries = member.shape[1]
    sum_keys = jnp.dot(
        member, back_keys.reshape(entries, spread * columns), preferred_element_type=jnp.float32
    )
    sum_values = jnp.dot(
        member, back_values.reshape(entries, spread * columns), preferred_element_type=jnp.float32
    )
    held_key_grad = sum_keys.astype(jnp.bfloat16).reshape(devices, tiles_here, spread, columns)
    held_value_grad = sum_values.astype(jnp.bfloat16).reshape(devices, tiles_here, spread, columns)
    owned_keys, owned_values = (
        lax.all_to_all(held_key_grad, "ctx", split_axis=0, concat_axis=2, tiled=True),
        lax.all_to_all(held_value_grad, "ctx", split_axis=0, concat_axis=2, tiled=True),
    )
    grad_key = (
        owned_keys.reshape(height, columns).astype(jnp.float32)
        + jnp.repeat(own_coarse_keys, POOL, axis=0) / POOL
    ).astype(jnp.bfloat16)
    grad_value = (
        owned_values.reshape(height, columns).astype(jnp.float32)
        + jnp.repeat(own_coarse_values, POOL, axis=0) / POOL
    ).astype(jnp.bfloat16)
    attended = out_tiles[0]
    grad_query = query_tiles[0]
    return (attended, grad_query, grad_key, grad_value, own_coarse_keys, own_coarse_values)


LANES = 128
JOBS = 4
SPLITS = 3
VMEM = pl.BlockSpec(memory_space=pltpu.VMEM)
SMEM = pl.BlockSpec(memory_space=pltpu.SMEM)
BIG = pltpu.CompilerParams(vmem_limit_bytes=50 * 1024 * 1024)


def nt(left, right):
    return contract(left, right, 1, 1)


def nn(left, right):
    return contract(left, right, 1, 0)


def split_rows(total):
    parts = []
    for _ in range(SPLITS):
        part = total.astype(jnp.bfloat16)
        parts.append(part.astype(jnp.float32))
        total = total - parts[-1]
    return parts


def tail_rows(coarse_key, coarse_value):
    per_tile = TILE // POOL
    parts = split_rows(jnp.concatenate([coarse_key, coarse_value], axis=0))
    used = SPLITS * 2 * per_tile
    filler = jnp.zeros((tail_height() - used, LANES), jnp.float32)
    return jnp.concatenate(parts + [filler], axis=0).astype(jnp.bfloat16)


def tail_height():
    used = SPLITS * 2 * (TILE // POOL)
    return -(-used // 16) * 16


def join_tail(tail):
    pair = 2 * (TILE // POOL)
    rows = tail.astype(jnp.float32)
    total = rows[:pair]
    for part in range(1, SPLITS):
        total = total + rows[part * pair : (part + 1) * pair]
    return total


def lane_block(index):
    return pl.ds(pl.multiple_of(index * LANES, LANES), LANES)


def pack_body(heads, span, place_ref, q_ref, k_ref, v_ref, g_ref, *out_refs):
    place = place_ref[0]
    for step, out_ref in enumerate(out_refs):
        if step < heads:
            head = lax.bitwise_xor(place, step)
        else:
            head = heads + lax.bitwise_xor(place // span, step - heads)
        for index, ref in enumerate((q_ref, k_ref, v_ref, g_ref)):
            out_ref[index * TILE : (index + 1) * TILE, :] = ref[:, lane_block(head)]


def pack(arrays, place, devices, span):
    return pl.pallas_call(
        functools.partial(pack_body, devices, span),
        in_specs=[SMEM] + [VMEM] * 4,
        out_specs=[VMEM] * HEADS,
        out_shape=[jax.ShapeDtypeStruct((4 * TILE, LANES), jnp.bfloat16)] * HEADS,
        compiler_params=BIG,
        cost_estimate=pl.CostEstimate(
            flops=0, transcendentals=0, bytes_accessed=16 * HEADS * TILE * LANES
        ),
        name="pack",
    )(place, *arrays)


def prepare(scratch):
    rows_ref, pool_key, pool_value, key_t, value_t, both_sum, pool_key_sum, pool_value_sum = scratch
    per_tile = TILE // POOL

    def one(tile, carry):
        for place, pool_ref, flip_ref in ((0, pool_key, key_t), (1, pool_value, value_t)):
            rows = rows_ref[tile, :, place * LANES : (place + 1) * LANES].astype(jnp.float32)
            means = [
                jnp.mean(rows[part * POOL : (part + 1) * POOL], axis=0, keepdims=True)
                for part in range(per_tile)
            ]
            pool_ref[pl.ds(tile * per_tile, per_tile), :] = jnp.concatenate(means, axis=0)
            flip_ref[tile] = rows.T.astype(jnp.bfloat16)
        both_sum[tile] = jnp.zeros((TILE, 2 * LANES), jnp.float32)
        return carry

    lax.fori_loop(0, rows_ref.shape[0], one, 0)
    pool_key_sum[...] = jnp.zeros_like(pool_key_sum)
    pool_value_sum[...] = jnp.zeros_like(pool_value_sum)


def wide_pair(left, right):
    zeros = jnp.zeros_like(left)
    return jnp.concatenate(
        [jnp.concatenate([left, zeros], axis=1), jnp.concatenate([zeros, right], axis=1)], axis=0
    )


def some_tiles(jobs, scratch, work):
    rows_ref, pool_key, pool_value, key_t, value_t, both_sum, pool_key_sum, pool_value_sum = scratch
    scaling = HEAD_DIM ** (-0.5)
    base2 = scaling * 1.4426950408889634
    comp = pool_key.shape[0]
    coarse_key = pool_key[...].astype(jnp.bfloat16)
    coarse_value = pool_value[...].astype(jnp.bfloat16)
    coarse = jnp.concatenate([coarse_key, coarse_value], axis=1)
    fine = SEL * TILE
    spans = [(slot * TILE, TILE) for slot in range(SEL)] + [(fine, comp)]
    results = []
    for (query, grad, listed), (score_ref, prob_ref, pair_ref) in zip(jobs, work):
        pair = wide_pair(query, grad)
        rows = [rows_ref[tile] for tile in listed]
        both = nt(jnp.concatenate(rows + [coarse], axis=0), pair)
        score_ref[...] = both[:, :LANES]
        prob_ref[...] = both[:, LANES:]
        top = jnp.max(both[:, :LANES], axis=0, keepdims=True)
        results.append((pair, top))
    for index, (_, (score_ref, prob_ref, pair_ref)) in enumerate(zip(jobs, work)):
        pair, top = results[index]
        raised = jnp.exp2((score_ref[...] - top) * base2)
        score_ref[...] = raised
        inverse = 1.0 / jnp.sum(raised, axis=0, keepdims=True)
        results[index] = (pair, inverse)
    outs = []
    for index, ((query, grad, listed), (score_ref, prob_ref, pair_ref)) in enumerate(zip(jobs, work)):
        pair, inverse = results[index]
        weight = score_ref[...] * inverse
        rounded = weight.astype(jnp.bfloat16)
        pair_ref[:, LANES:] = rounded
        score_ref[...] = weight
        values_t = jnp.concatenate([value_t[tile] for tile in listed], axis=1)
        out_t = nn(values_t, pair_ref[:fine, LANES:]) + contract(
            coarse_value, pair_ref[fine:, LANES:], 0, 0
        )
        out_t = out_t.astype(jnp.bfloat16).astype(jnp.float32)
        dots = jnp.sum(out_t * grad.astype(jnp.float32).T, axis=0, keepdims=True)
        outs.append((out_t, dots))
    for index, ((query, grad, listed), (score_ref, prob_ref, pair_ref)) in enumerate(zip(jobs, work)):
        out_t, dots = outs[index]
        slope = (score_ref[...] * (prob_ref[...] - dots)).astype(jnp.bfloat16)
        pair_ref[:, :LANES] = slope
        terms = nn(pair_ref[...], results[index][0])
        for tile, (start, size) in zip(listed, spans):
            both_sum[tile] += terms[start : start + size]
        pool_key_sum[...] += terms[fine:, :LANES]
        pool_value_sum[...] += terms[fine:, LANES:]
        keys_t = jnp.concatenate([key_t[tile] for tile in listed], axis=1)
        query_t = nn(keys_t, pair_ref[:fine, :LANES]) + contract(
            coarse_key, pair_ref[fine:, :LANES], 0, 0
        )
        outs[index] = (
            out_t.T.astype(jnp.bfloat16),
            (query_t.T * scaling).astype(jnp.bfloat16),
        )
    return outs


def finish(tile, scratch):
    scaling = HEAD_DIM ** (-0.5)
    both_sum, pool_key_sum, pool_value_sum = scratch
    per_tile = TILE // POOL
    coarse_key = pool_key_sum[pl.ds(tile * per_tile, per_tile), :] * scaling
    coarse_value = pool_value_sum[pl.ds(tile * per_tile, per_tile), :]

    def whole(fine, coarse):
        return jnp.concatenate(
            [
                fine[part * POOL : (part + 1) * POOL] + coarse[part : part + 1] * (1.0 / POOL)
                for part in range(per_tile)
            ],
            axis=0,
        )

    return (
        whole(both_sum[tile, :, :LANES] * scaling, coarse_key),
        whole(both_sum[tile, :, LANES:], coarse_value),
        coarse_key,
        coarse_value,
    )


def head_scratch(tiles):
    comp = tiles * (TILE // POOL)
    keys = SEL * TILE + comp
    return [
        pltpu.VMEM((tiles, TILE, 2 * LANES), jnp.bfloat16),
        pltpu.VMEM((comp, LANES), jnp.float32),
        pltpu.VMEM((comp, LANES), jnp.float32),
        pltpu.VMEM((tiles, LANES, TILE), jnp.bfloat16),
        pltpu.VMEM((tiles, LANES, TILE), jnp.bfloat16),
        pltpu.VMEM((tiles, TILE, 2 * LANES), jnp.float32),
        pltpu.VMEM((comp, LANES), jnp.float32),
        pltpu.VMEM((comp, LANES), jnp.float32),
    ] + JOBS * [
        pltpu.VMEM((keys, LANES), jnp.float32),
        pltpu.VMEM((keys, LANES), jnp.float32),
        pltpu.VMEM((keys, 2 * LANES), jnp.bfloat16),
    ]


def split_scratch(scratch):
    totals, work = scratch[:8], scratch[8:]
    return totals, [work[3 * job : 3 * job + 3] for job in range(JOBS)]


def head_cost(queries, keys, moved):
    return pl.CostEstimate(
        flops=12 * queries * keys * LANES,
        transcendentals=queries * keys,
        bytes_accessed=moved,
    )


def every_tile(count, stride, place_ref, sel_ref, query_ref, out_ref, totals, work):
    place = place_ref[0]

    def some(first, carry):
        jobs = []
        for job in range(JOBS):
            piece = first * JOBS + job
            tile = lax.bitwise_xor(place, piece * stride)
            listed = [lax.bitwise_xor(sel_ref[tile, slot], place) for slot in range(SEL)]
            jobs.append((query_ref[piece, :, :LANES], query_ref[piece, :, LANES:], listed))
        for job, (rows, slopes) in enumerate(some_tiles(jobs, totals, work)):
            out_ref[first * JOBS + job, :TILE, :] = rows
            out_ref[first * JOBS + job, TILE : 2 * TILE, :] = slopes
        return carry

    lax.fori_loop(0, count // JOBS, some, 0)


def whole_head(tiles, place_ref, sel_ref, *refs):
    pieces, outs = refs[:tiles][::-1], refs[tiles : 2 * tiles]
    query_ref, out_ref = refs[2 * tiles : 2 * tiles + 2]
    totals, work = split_scratch(refs[2 * tiles + 2 :])
    for step, piece in enumerate(pieces):
        query_ref[step, :, :LANES] = piece[:TILE, :]
        totals[0][step, :, :LANES] = piece[TILE : 2 * TILE, :]
        totals[0][step, :, LANES:] = piece[2 * TILE : 3 * TILE, :]
        query_ref[step, :, LANES:] = piece[3 * TILE :, :]
    prepare(totals)
    every_tile(tiles, 1, place_ref, sel_ref, query_ref, out_ref, totals, work)
    for step, out in enumerate(outs):
        key, value, coarse_key, coarse_value = finish(step, totals[5:])
        out[: 2 * TILE, :] = out_ref[step]
        out[2 * TILE : 3 * TILE, :] = key.astype(jnp.bfloat16)
        out[3 * TILE : 4 * TILE, :] = value.astype(jnp.bfloat16)
        out[4 * TILE :, :] = tail_rows(coarse_key, coarse_value)


def shared_head(span, planes, place_ref, sel_ref, *refs):
    owns, refs = refs[:planes], refs[planes:]
    pieces, refs = refs[: span - 1], refs[span - 1 :]
    out_ref, keep_ref = refs[:2]
    send_refs = refs[2 : span + 1]
    query_ref = refs[span + 1]
    totals, work = split_scratch(refs[span + 2 :])
    for plane, own in enumerate(owns):
        query_ref[plane, :, :LANES] = own[:TILE, :]
        query_ref[plane, :, LANES:] = own[3 * TILE :, :]
        totals[0][plane * span, :, :LANES] = own[TILE : 2 * TILE, :]
        totals[0][plane * span, :, LANES:] = own[2 * TILE : 3 * TILE, :]
        for step in range(1, span):
            piece = pieces[step - 1]
            totals[0][plane * span + step, :, :LANES] = piece[plane, :TILE, :]
            totals[0][plane * span + step, :, LANES:] = piece[plane, TILE:, :]
    prepare(totals)
    every_tile(planes, span, place_ref, sel_ref, query_ref, out_ref, totals, work)
    for step in range(span):

        def last(plane, carry, step=step):
            key, value, coarse_key, coarse_value = finish(plane * span + step, totals[5:])
            if step == 0:
                pair = 2 * (TILE // POOL)
                keep_ref[plane, :TILE, :] = key
                keep_ref[plane, TILE : 2 * TILE, :] = value
                keep_ref[plane, 2 * TILE : 2 * TILE + 8, :] = jnp.concatenate(
                    [coarse_key, coarse_value, jnp.zeros((8 - pair, LANES), jnp.float32)], axis=0
                )
            else:
                ref = send_refs[step - 1]
                ref[plane, :TILE, :] = key.astype(jnp.bfloat16)
                ref[plane, TILE : 2 * TILE, :] = value.astype(jnp.bfloat16)
                ref[plane, 2 * TILE :, :] = tail_rows(coarse_key, coarse_value)
            return carry

        lax.fori_loop(0, planes, last, 0)


def gather_terms(span, rows_ref, keep_ref, *refs):
    pieces, outs = refs[: span - 1], refs[span - 1 :]
    per_tile = TILE // POOL
    for plane, out in enumerate(outs):
        fine = keep_ref[plane, : 2 * TILE, :]
        coarse = keep_ref[plane, 2 * TILE : 2 * TILE + 2 * per_tile, :]
        for piece in pieces:
            fine = fine + piece[plane, : 2 * TILE, :].astype(jnp.float32)
            coarse = coarse + join_tail(piece[plane, 2 * TILE :, :])
        out[: 2 * TILE, :] = rows_ref[plane]
        out[2 * TILE : 4 * TILE, :] = fine.astype(jnp.bfloat16)
        out[4 * TILE :, :] = tail_rows(coarse[:per_tile], coarse[per_tile:])


def unpack_body(heads, span, place_ref, *refs):
    pieces, (a_ref, q_ref, k_ref, v_ref, pk_ref, pv_ref) = refs[:-6], refs[-6:]
    pieces = pieces[:heads][::-1] + pieces[heads:][::-1]
    per_tile = TILE // POOL
    place = place_ref[0]
    for step, ref in enumerate(pieces):
        if step < heads:
            head = lax.bitwise_xor(place, step)
        else:
            head = heads + lax.bitwise_xor(place // span, step - heads)
        columns = lane_block(head)
        for index, out in enumerate((a_ref, q_ref, k_ref, v_ref)):
            out[:, columns] = ref[index * TILE : (index + 1) * TILE, :]
        coarse = join_tail(ref[4 * TILE :, :])
        pk_ref[:, columns] = coarse[:per_tile]
        pv_ref[:, columns] = coarse[per_tile:]


def head_shards(query_rows, key_rows, value_rows, out_grad, selected):
    devices = lax.axis_size("ctx")
    height, columns = query_rows.shape
    planes = HEADS - devices
    span = devices // planes
    arrays = (query_rows, key_rows, value_rows, out_grad)
    place = jnp.reshape(lax.axis_index("ctx"), (1,))

    def shift(block, step):
        return lax.ppermute(block, "ctx", [(i, i ^ step) for i in range(devices)])

    def spread(pieces, stride):
        moved = [pieces[0]]
        for step in range(1, len(pieces)):
            moved.append(shift(pieces[step], step * stride))
        return moved

    def shape(*dims, dtype=jnp.bfloat16):
        return jax.ShapeDtypeStruct(dims, dtype)

    block = 4 * TILE + tail_height()
    part = 2 * TILE + tail_height()
    keys = SEL * TILE + devices * (TILE // POOL)
    packed = pack(arrays, place, devices, span)
    owns = spread(packed[devices:], span)
    mains = spread(packed[:devices], 1)
    own_kv = jnp.stack([own[TILE : 3 * TILE] for own in owns])
    pieces = [shift(own_kv, step) for step in range(1, span)]
    outs = pl.pallas_call(
        functools.partial(shared_head, span, planes),
        in_specs=[SMEM, SMEM] + [VMEM] * (planes + span - 1),
        out_specs=[VMEM] * (span + 1),
        out_shape=[
            shape(planes, 2 * TILE, LANES),
            shape(planes, 2 * TILE + 8, LANES, dtype=jnp.float32),
        ]
        + [shape(planes, part, LANES)] * (span - 1),
        scratch_shapes=[pltpu.VMEM((planes, TILE, 2 * LANES), jnp.bfloat16)]
        + head_scratch(devices),
        compiler_params=BIG,
        cost_estimate=head_cost(planes * TILE, keys, 16 * devices * TILE * LANES),
        name="shared_head",
    )(place, selected, *owns, *pieces)
    terms = [shift(sent, step + 1) for step, sent in enumerate(outs[2:])]
    rests = pl.pallas_call(
        functools.partial(gather_terms, span),
        in_specs=[VMEM] * (span + 1),
        out_specs=[VMEM] * planes,
        out_shape=[shape(block, LANES)] * planes,
        compiler_params=BIG,
        name="gather_terms",
    )(outs[0], outs[1], *terms)
    rests = spread(rests, span)
    dones = pl.pallas_call(
        functools.partial(whole_head, devices),
        in_specs=[SMEM, SMEM] + [VMEM] * devices,
        out_specs=[VMEM] * devices,
        out_shape=[shape(block, LANES)] * devices,
        scratch_shapes=[
            pltpu.VMEM((devices, TILE, 2 * LANES), jnp.bfloat16),
            pltpu.VMEM((devices, 2 * TILE, LANES), jnp.bfloat16),
        ]
        + head_scratch(devices),
        compiler_params=BIG,
        cost_estimate=head_cost(devices * TILE, keys, 16 * devices * TILE * LANES),
        name="whole_head",
    )(place, selected, *mains[::-1])
    dones = spread(dones, 1)
    wide = shape(height, columns)
    thin = shape(height // POOL, columns, dtype=jnp.float32)
    return pl.pallas_call(
        functools.partial(unpack_body, devices, span),
        in_specs=[SMEM] + [VMEM] * HEADS,
        out_specs=[VMEM] * 6,
        out_shape=[wide, wide, wide, wide, thin, thin],
        compiler_params=BIG,
        name="unpack",
    )(place, *dones[::-1], *rests[::-1])


def shards(query_rows, key_rows, value_rows, out_grad, selected):
    devices = lax.axis_size("ctx")
    planes = HEADS - devices
    tiles_here = query_rows.shape[0] // TILE
    if planes > 0 and devices % planes == 0 and tiles_here == 1 and planes % JOBS == 0:
        span = devices // planes
        if span & (span - 1) == 0:
            return head_shards(query_rows, key_rows, value_rows, out_grad, selected)
    return listed_shards(query_rows, key_rows, value_rows, out_grad, selected)


def solution(mesh):
    in_specs = (
        P(("groups", "ctx"), None),
        P(("groups", "ctx"), None),
        P(("groups", "ctx"), None),
        P(("groups", "ctx"), None),
        P("groups", None),
    )
    out_specs = (
        P(("groups", "ctx"), None),
        P(("groups", "ctx"), None),
        P(("groups", "ctx"), None),
        P(("groups", "ctx"), None),
        P(("groups", "ctx"), None),
        P(("groups", "ctx"), None),
    )
    return jax.shard_map(
        shards, mesh=mesh, in_specs=in_specs, out_specs=out_specs, check_vma=False
    )
```

```python
import functools

import jax
import jax.numpy as jnp
from jax import lax
from jax.experimental import pallas as pl
from jax.experimental.pallas import tpu as pltpu
from jax.sharding import PartitionSpec as P


HEADS = 20
HEAD_DIM = 128
TILE = 128
POOL = 64
SEL = 8


def pooled(rows):
    return jnp.mean(rows.astype(jnp.float32).reshape(-1, POOL, rows.shape[1]), axis=1).astype(
        jnp.bfloat16
    )


def contract(left, right, left_dim, right_dim):
    return lax.dot_general(
        left, right, (((left_dim,), (right_dim,)), ((), ())), preferred_element_type=jnp.float32
    )


def attend(queries, grads_out, keys_all, values_all):
    scaling = HEAD_DIM ** (-0.5)
    out_parts, query_parts, key_parts, value_parts = ([], [], [], [])
    for head in range(HEADS):
        lower = head * HEAD_DIM
        upper = lower + HEAD_DIM
        head_query = queries[:, lower:upper]
        head_grad = grads_out[:, lower:upper]
        head_key = keys_all[:, lower:upper]
        head_value = values_all[:, lower:upper]
        scores = contract(head_query, head_key, 1, 1) * scaling
        summit = jnp.max(scores, axis=-1, keepdims=True)
        raised = jnp.exp(scores - summit)
        weights = raised / jnp.sum(raised, axis=-1, keepdims=True)
        rounded = weights.astype(jnp.bfloat16)
        out_rows = jnp.dot(rounded, head_value, preferred_element_type=jnp.float32).astype(
            jnp.bfloat16
        )
        row_dots = jnp.sum(
            head_grad.astype(jnp.float32) * out_rows.astype(jnp.float32), axis=-1, keepdims=True
        )
        prob_grad = contract(head_grad, head_value, 1, 1)
        score_grad = (weights * (prob_grad - row_dots)).astype(jnp.bfloat16)
        query_grad = jnp.dot(score_grad, head_key, preferred_element_type=jnp.float32) * scaling
        key_terms = contract(score_grad, head_query, 0, 0) * scaling
        value_terms = contract(rounded, head_grad, 0, 0)
        out_parts.append(out_rows)
        query_parts.append(query_grad.astype(jnp.bfloat16))
        key_parts.append(key_terms)
        value_parts.append(value_terms)
    return (
        jnp.concatenate(out_parts, axis=1),
        jnp.concatenate(query_parts, axis=1),
        jnp.concatenate(key_parts, axis=1),
        jnp.concatenate(value_parts, axis=1),
    )


def package(tiles_in, pooled_in, devices, spread):
    tiles_here, tile_len, columns = tiles_in.shape
    per_tile = tile_len // POOL
    split_rows = tiles_in.reshape(tiles_here, devices, spread, columns)
    copies = jnp.broadcast_to(
        pooled_in.reshape(tiles_here, 1, per_tile, columns),
        (tiles_here, devices, per_tile, columns),
    )
    return jnp.concatenate([split_rows, copies], axis=2).reshape(
        tiles_here, devices * (spread + per_tile), columns
    )


def listed_shards(query_rows, key_rows, value_rows, out_grad, selected):
    height, columns = query_rows.shape
    devices = lax.axis_size("ctx")
    tiles_here = height // TILE
    spread = TILE // devices
    own_keys = pooled(key_rows)
    own_values = pooled(value_rows)
    key_tiles = key_rows.reshape(tiles_here, TILE, columns)
    value_tiles = value_rows.reshape(tiles_here, TILE, columns)
    joined_keys, joined_values = (
        lax.all_to_all(
            package(key_tiles, own_keys, devices, spread),
            "ctx",
            split_axis=1,
            concat_axis=0,
            tiled=True,
        ),
        lax.all_to_all(
            package(value_tiles, own_values, devices, spread),
            "ctx",
            split_axis=1,
            concat_axis=0,
            tiled=True,
        ),
    )
    held_keys = joined_keys[:, :spread]
    held_values = joined_values[:, :spread]
    pool_keys = joined_keys[:, spread:].reshape(-1, columns)
    pool_values = joined_values[:, spread:].reshape(-1, columns)
    comp_count = pool_keys.shape[0]
    got_keys, got_values = (
        lax.all_to_all(held_keys[selected], "ctx", split_axis=0, concat_axis=2, tiled=True),
        lax.all_to_all(held_values[selected], "ctx", split_axis=0, concat_axis=2, tiled=True),
    )
    fine_keys = got_keys.reshape(tiles_here, SEL * TILE, columns)
    fine_values = got_values.reshape(tiles_here, SEL * TILE, columns)
    out_tiles, query_tiles, key_listed, value_listed = ([], [], [], [])
    keys_all = jnp.concatenate([pool_keys, fine_keys[0]], axis=0)
    values_all = jnp.concatenate([pool_values, fine_values[0]], axis=0)
    out_rows, query_grad, key_terms, value_terms = attend(
        query_rows, out_grad, keys_all, values_all
    )
    out_tiles.append(out_rows)
    query_tiles.append(query_grad)
    coarse_keys = key_terms[:comp_count]
    coarse_values = value_terms[:comp_count]
    key_listed.append(key_terms[comp_count:].astype(jnp.bfloat16))
    value_listed.append(value_terms[comp_count:].astype(jnp.bfloat16))
    own_coarse_keys, own_coarse_values = (
        lax.psum_scatter(coarse_keys, "ctx", scatter_dimension=0, tiled=True),
        lax.psum_scatter(coarse_values, "ctx", scatter_dimension=0, tiled=True),
    )
    listed_keys = jnp.stack(key_listed).reshape(tiles_here * SEL, devices, spread, columns)
    listed_values = jnp.stack(value_listed).reshape(tiles_here * SEL, devices, spread, columns)
    back_keys, back_values = (
        lax.all_to_all(listed_keys, "ctx", split_axis=1, concat_axis=0, tiled=True),
        lax.all_to_all(listed_values, "ctx", split_axis=1, concat_axis=0, tiled=True),
    )
    tile_ids = jnp.arange(selected.shape[0], dtype=jnp.int32)[:, None]
    member = (selected.reshape(1, -1) == tile_ids).astype(jnp.bfloat16)
    entries = member.shape[1]
    sum_keys = jnp.dot(
        member, back_keys.reshape(entries, spread * columns), preferred_element_type=jnp.float32
    )
    sum_values = jnp.dot(
        member, back_values.reshape(entries, spread * columns), preferred_element_type=jnp.float32
    )
    held_key_grad = sum_keys.astype(jnp.bfloat16).reshape(devices, tiles_here, spread, columns)
    held_value_grad = sum_values.astype(jnp.bfloat16).reshape(devices, tiles_here, spread, columns)
    owned_keys, owned_values = (
        lax.all_to_all(held_key_grad, "ctx", split_axis=0, concat_axis=2, tiled=True),
        lax.all_to_all(held_value_grad, "ctx", split_axis=0, concat_axis=2, tiled=True),
    )
    grad_key = (
        owned_keys.reshape(height, columns).astype(jnp.float32)
        + jnp.repeat(own_coarse_keys, POOL, axis=0) / POOL
    ).astype(jnp.bfloat16)
    grad_value = (
        owned_values.reshape(height, columns).astype(jnp.float32)
        + jnp.repeat(own_coarse_values, POOL, axis=0) / POOL
    ).astype(jnp.bfloat16)
    attended = out_tiles[0]
    grad_query = query_tiles[0]
    return (attended, grad_query, grad_key, grad_value, own_coarse_keys, own_coarse_values)


LANES = 128
JOBS = 4
SPLITS = 3
VMEM = pl.BlockSpec(memory_space=pltpu.VMEM)
SMEM = pl.BlockSpec(memory_space=pltpu.SMEM)
BIG = pltpu.CompilerParams(vmem_limit_bytes=50 * 1024 * 1024)


def nt(left, right):
    return contract(left, right, 1, 1)


def nn(left, right):
    return contract(left, right, 1, 0)


def split_rows(total):
    parts = []
    for _ in range(SPLITS):
        part = total.astype(jnp.bfloat16)
        parts.append(part.astype(jnp.float32))
        total = total - parts[-1]
    return parts


def tail_rows(coarse_key, coarse_value):
    per_tile = TILE // POOL
    parts = split_rows(jnp.concatenate([coarse_key, coarse_value], axis=0))
    used = SPLITS * 2 * per_tile
    filler = jnp.zeros((tail_height() - used, LANES), jnp.float32)
    return jnp.concatenate(parts + [filler], axis=0).astype(jnp.bfloat16)


def tail_height():
    used = SPLITS * 2 * (TILE // POOL)
    return -(-used // 16) * 16


def join_tail(tail):
    pair = 2 * (TILE // POOL)
    rows = tail.astype(jnp.float32)
    total = rows[:pair]
    for part in range(1, SPLITS):
        total = total + rows[part * pair : (part + 1) * pair]
    return total


def lane_block(index):
    return pl.ds(pl.multiple_of(index * LANES, LANES), LANES)


def pack_body(first, place_ref, q_ref, k_ref, v_ref, g_ref, *out_refs):
    for step, out_ref in enumerate(out_refs):
        columns = lane_block(first + lax.bitwise_xor(place_ref[0], step))
        for index, ref in enumerate((q_ref, k_ref, v_ref, g_ref)):
            out_ref[index * TILE : (index + 1) * TILE, :] = ref[:, columns]


def pack(arrays, place, first, count):
    width = arrays[0].shape[1]
    if first % count == 0:
        spec = pl.BlockSpec((TILE, count * LANES), lambda i, _: (0, first // count))
        start = 0
    else:
        spec = pl.BlockSpec((TILE, width), lambda i, _: (0, 0))
        start = first
    out = pl.BlockSpec((4 * TILE, LANES), lambda i, _: (0, 0))
    return pl.pallas_call(
        functools.partial(pack_body, start),
        grid_spec=pltpu.PrefetchScalarGridSpec(
            num_scalar_prefetch=1, grid=(1,), in_specs=[spec] * 4, out_specs=[out] * count
        ),
        out_shape=[jax.ShapeDtypeStruct((4 * TILE, LANES), jnp.bfloat16)] * count,
        cost_estimate=pl.CostEstimate(
            flops=0, transcendentals=0, bytes_accessed=16 * count * TILE * LANES
        ),
        name="pack",
    )(place, *arrays)


def prepare(scratch):
    rows_ref, pool_key, pool_value, key_t, value_t, both_sum, pool_key_sum, pool_value_sum = scratch
    per_tile = TILE // POOL

    def one(tile, carry):
        for place, pool_ref, flip_ref in ((0, pool_key, key_t), (1, pool_value, value_t)):
            rows = rows_ref[tile, :, place * LANES : (place + 1) * LANES].astype(jnp.float32)
            means = [
                jnp.mean(rows[part * POOL : (part + 1) * POOL], axis=0, keepdims=True)
                for part in range(per_tile)
            ]
            pool_ref[pl.ds(tile * per_tile, per_tile), :] = jnp.concatenate(means, axis=0)
            flip_ref[tile] = rows.T.astype(jnp.bfloat16)
        both_sum[tile] = jnp.zeros((TILE, 2 * LANES), jnp.float32)
        return carry

    lax.fori_loop(0, rows_ref.shape[0], one, 0)
    pool_key_sum[...] = jnp.zeros_like(pool_key_sum)
    pool_value_sum[...] = jnp.zeros_like(pool_value_sum)


def wide_pair(left, right):
    zeros = jnp.zeros_like(left)
    return jnp.concatenate(
        [jnp.concatenate([left, zeros], axis=1), jnp.concatenate([zeros, right], axis=1)], axis=0
    )


def some_tiles(jobs, scratch, work):
    rows_ref, pool_key, pool_value, key_t, value_t, both_sum, pool_key_sum, pool_value_sum = scratch
    scaling = HEAD_DIM ** (-0.5)
    base2 = scaling * 1.4426950408889634
    comp = pool_key.shape[0]
    coarse_key = pool_key[...].astype(jnp.bfloat16)
    coarse_value = pool_value[...].astype(jnp.bfloat16)
    coarse = jnp.concatenate([coarse_key, coarse_value], axis=1)
    fine = SEL * TILE
    spans = [(slot * TILE, TILE) for slot in range(SEL)] + [(fine, comp)]
    results = []
    for (query, grad, listed), (score_ref, prob_ref, pair_ref) in zip(jobs, work):
        pair = wide_pair(query, grad)
        rows = [rows_ref[tile] for tile in listed]
        both = nt(jnp.concatenate(rows + [coarse], axis=0), pair)
        score_ref[...] = both[:, :LANES]
        prob_ref[...] = both[:, LANES:]
        top = jnp.max(both[:, :LANES], axis=0, keepdims=True)
        results.append((pair, top))
    for index, (_, (score_ref, prob_ref, pair_ref)) in enumerate(zip(jobs, work)):
        pair, top = results[index]
        raised = jnp.exp2((score_ref[...] - top) * base2)
        score_ref[...] = raised
        inverse = 1.0 / jnp.sum(raised, axis=0, keepdims=True)
        results[index] = (pair, inverse)
    outs = []
    for index, ((query, grad, listed), (score_ref, prob_ref, pair_ref)) in enumerate(zip(jobs, work)):
        pair, inverse = results[index]
        weight = score_ref[...] * inverse
        rounded = weight.astype(jnp.bfloat16)
        pair_ref[:, LANES:] = rounded
        score_ref[...] = weight
        values_t = jnp.concatenate([value_t[tile] for tile in listed], axis=1)
        out_t = nn(values_t, pair_ref[:fine, LANES:]) + contract(
            coarse_value, pair_ref[fine:, LANES:], 0, 0
        )
        out_t = out_t.astype(jnp.bfloat16).astype(jnp.float32)
        dots = jnp.sum(out_t * grad.astype(jnp.float32).T, axis=0, keepdims=True)
        outs.append((out_t, dots))
    for index, ((query, grad, listed), (score_ref, prob_ref, pair_ref)) in enumerate(zip(jobs, work)):
        out_t, dots = outs[index]
        slope = (score_ref[...] * (prob_ref[...] - dots)).astype(jnp.bfloat16)
        pair_ref[:, :LANES] = slope
        terms = nn(pair_ref[...], results[index][0])
        for tile, (start, size) in zip(listed, spans):
            both_sum[tile] += terms[start : start + size]
        pool_key_sum[...] += terms[fine:, :LANES]
        pool_value_sum[...] += terms[fine:, LANES:]
        keys_t = jnp.concatenate([key_t[tile] for tile in listed], axis=1)
        query_t = nn(keys_t, pair_ref[:fine, :LANES]) + contract(
            coarse_key, pair_ref[fine:, :LANES], 0, 0
        )
        outs[index] = (
            out_t.T.astype(jnp.bfloat16),
            (query_t.T * scaling).astype(jnp.bfloat16),
        )
    return outs


def finish(tile, scratch):
    scaling = HEAD_DIM ** (-0.5)
    both_sum, pool_key_sum, pool_value_sum = scratch
    per_tile = TILE // POOL
    coarse_key = pool_key_sum[pl.ds(tile * per_tile, per_tile), :] * scaling
    coarse_value = pool_value_sum[pl.ds(tile * per_tile, per_tile), :]

    def whole(fine, coarse):
        return jnp.concatenate(
            [
                fine[part * POOL : (part + 1) * POOL] + coarse[part : part + 1] * (1.0 / POOL)
                for part in range(per_tile)
            ],
            axis=0,
        )

    return (
        whole(both_sum[tile, :, :LANES] * scaling, coarse_key),
        whole(both_sum[tile, :, LANES:], coarse_value),
        coarse_key,
        coarse_value,
    )


def head_scratch(tiles):
    comp = tiles * (TILE // POOL)
    keys = SEL * TILE + comp
    return [
        pltpu.VMEM((tiles, TILE, 2 * LANES), jnp.bfloat16),
        pltpu.VMEM((comp, LANES), jnp.float32),
        pltpu.VMEM((comp, LANES), jnp.float32),
        pltpu.VMEM((tiles, LANES, TILE), jnp.bfloat16),
        pltpu.VMEM((tiles, LANES, TILE), jnp.bfloat16),
        pltpu.VMEM((tiles, TILE, 2 * LANES), jnp.float32),
        pltpu.VMEM((comp, LANES), jnp.float32),
        pltpu.VMEM((comp, LANES), jnp.float32),
    ] + JOBS * [
        pltpu.VMEM((keys, LANES), jnp.float32),
        pltpu.VMEM((keys, LANES), jnp.float32),
        pltpu.VMEM((keys, 2 * LANES), jnp.bfloat16),
    ]


def split_scratch(scratch):
    totals, work = scratch[:8], scratch[8:]
    return totals, [work[3 * job : 3 * job + 3] for job in range(JOBS)]


def head_cost(queries, keys, moved):
    return pl.CostEstimate(
        flops=12 * queries * keys * LANES,
        transcendentals=queries * keys,
        bytes_accessed=moved,
    )


def every_tile(count, stride, place_ref, sel_ref, query_ref, out_ref, totals, work):
    place = place_ref[0]

    def some(first, carry):
        jobs = []
        for job in range(JOBS):
            piece = first * JOBS + job
            tile = lax.bitwise_xor(place, piece * stride)
            listed = [lax.bitwise_xor(sel_ref[tile, slot], place) for slot in range(SEL)]
            jobs.append((query_ref[piece, :, :LANES], query_ref[piece, :, LANES:], listed))
        for job, (rows, slopes) in enumerate(some_tiles(jobs, totals, work)):
            out_ref[first * JOBS + job, :TILE, :] = rows
            out_ref[first * JOBS + job, TILE : 2 * TILE, :] = slopes
        return carry

    lax.fori_loop(0, count // JOBS, some, 0)


def whole_head(tiles, place_ref, sel_ref, *refs):
    pieces, outs = refs[:tiles][::-1], refs[tiles : 2 * tiles]
    query_ref, out_ref = refs[2 * tiles : 2 * tiles + 2]
    totals, work = split_scratch(refs[2 * tiles + 2 :])
    for step, piece in enumerate(pieces):
        query_ref[step, :, :LANES] = piece[:TILE, :]
        totals[0][step, :, :LANES] = piece[TILE : 2 * TILE, :]
        totals[0][step, :, LANES:] = piece[2 * TILE : 3 * TILE, :]
        query_ref[step, :, LANES:] = piece[3 * TILE :, :]
    prepare(totals)
    every_tile(tiles, 1, place_ref, sel_ref, query_ref, out_ref, totals, work)
    for step, out in enumerate(outs):
        key, value, coarse_key, coarse_value = finish(step, totals[5:])
        out[: 2 * TILE, :] = out_ref[step]
        out[2 * TILE : 3 * TILE, :] = key.astype(jnp.bfloat16)
        out[3 * TILE : 4 * TILE, :] = value.astype(jnp.bfloat16)
        out[4 * TILE :, :] = tail_rows(coarse_key, coarse_value)


def shared_head(span, planes, place_ref, sel_ref, *refs):
    owns, refs = refs[:planes], refs[planes:]
    pieces, refs = refs[: span - 1], refs[span - 1 :]
    out_ref, keep_ref = refs[:2]
    send_refs = refs[2 : span + 1]
    query_ref = refs[span + 1]
    totals, work = split_scratch(refs[span + 2 :])
    for plane, own in enumerate(owns):
        query_ref[plane, :, :LANES] = own[:TILE, :]
        query_ref[plane, :, LANES:] = own[3 * TILE :, :]
        totals[0][plane * span, :, :LANES] = own[TILE : 2 * TILE, :]
        totals[0][plane * span, :, LANES:] = own[2 * TILE : 3 * TILE, :]
        for step in range(1, span):
            piece = pieces[step - 1]
            totals[0][plane * span + step, :, :LANES] = piece[plane, :TILE, :]
            totals[0][plane * span + step, :, LANES:] = piece[plane, TILE:, :]
    prepare(totals)
    every_tile(planes, span, place_ref, sel_ref, query_ref, out_ref, totals, work)
    for step in range(span):

        def last(plane, carry, step=step):
            key, value, coarse_key, coarse_value = finish(plane * span + step, totals[5:])
            if step == 0:
                pair = 2 * (TILE // POOL)
                keep_ref[plane, :TILE, :] = key
                keep_ref[plane, TILE : 2 * TILE, :] = value
                keep_ref[plane, 2 * TILE : 2 * TILE + 8, :] = jnp.concatenate(
                    [coarse_key, coarse_value, jnp.zeros((8 - pair, LANES), jnp.float32)], axis=0
                )
            else:
                ref = send_refs[step - 1]
                ref[plane, :TILE, :] = key.astype(jnp.bfloat16)
                ref[plane, TILE : 2 * TILE, :] = value.astype(jnp.bfloat16)
                ref[plane, 2 * TILE :, :] = tail_rows(coarse_key, coarse_value)
            return carry

        lax.fori_loop(0, planes, last, 0)


def gather_terms(span, rows_ref, keep_ref, *refs):
    pieces, outs = refs[: span - 1], refs[span - 1 :]
    per_tile = TILE // POOL
    for plane, out in enumerate(outs):
        fine = keep_ref[plane, : 2 * TILE, :]
        coarse = keep_ref[plane, 2 * TILE : 2 * TILE + 2 * per_tile, :]
        for piece in pieces:
            fine = fine + piece[plane, : 2 * TILE, :].astype(jnp.float32)
            coarse = coarse + join_tail(piece[plane, 2 * TILE :, :])
        out[: 2 * TILE, :] = rows_ref[plane]
        out[2 * TILE : 4 * TILE, :] = fine.astype(jnp.bfloat16)
        out[4 * TILE :, :] = tail_rows(coarse[:per_tile], coarse[per_tile:])


def unpack_body(heads, span, place_ref, *refs):
    pieces, (a_ref, q_ref, k_ref, v_ref, pk_ref, pv_ref) = refs[:-6], refs[-6:]
    pieces = pieces[:heads][::-1] + pieces[heads:][::-1]
    per_tile = TILE // POOL
    place = place_ref[0]
    for step, ref in enumerate(pieces):
        if step < heads:
            head = lax.bitwise_xor(place, step)
        else:
            head = heads + lax.bitwise_xor(place // span, step - heads)
        columns = lane_block(head)
        for index, out in enumerate((a_ref, q_ref, k_ref, v_ref)):
            out[:, columns] = ref[index * TILE : (index + 1) * TILE, :]
        coarse = join_tail(ref[4 * TILE :, :])
        pk_ref[:, columns] = coarse[:per_tile]
        pv_ref[:, columns] = coarse[per_tile:]


def head_shards(query_rows, key_rows, value_rows, out_grad, selected):
    devices = lax.axis_size("ctx")
    height, columns = query_rows.shape
    planes = HEADS - devices
    span = devices // planes
    arrays = (query_rows, key_rows, value_rows, out_grad)
    place = jnp.reshape(lax.axis_index("ctx"), (1,))

    def shift(block, step):
        return lax.ppermute(block, "ctx", [(i, i ^ step) for i in range(devices)])

    def spread(pieces, stride):
        moved = [pieces[0]]
        for step in range(1, len(pieces)):
            moved.append(shift(pieces[step], step * stride))
        return moved

    def shape(*dims, dtype=jnp.bfloat16):
        return jax.ShapeDtypeStruct(dims, dtype)

    block = 4 * TILE + tail_height()
    part = 2 * TILE + tail_height()
    keys = SEL * TILE + devices * (TILE // POOL)
    owns = spread(pack(arrays, place // span, devices, planes), span)
    mains = spread(pack(arrays, place, 0, devices), 1)
    own_kv = jnp.stack([own[TILE : 3 * TILE] for own in owns])
    pieces = [shift(own_kv, step) for step in range(1, span)]
    outs = pl.pallas_call(
        functools.partial(shared_head, span, planes),
        in_specs=[SMEM, SMEM] + [VMEM] * (planes + span - 1),
        out_specs=[VMEM] * (span + 1),
        out_shape=[
            shape(planes, 2 * TILE, LANES),
            shape(planes, 2 * TILE + 8, LANES, dtype=jnp.float32),
        ]
        + [shape(planes, part, LANES)] * (span - 1),
        scratch_shapes=[pltpu.VMEM((planes, TILE, 2 * LANES), jnp.bfloat16)]
        + head_scratch(devices),
        compiler_params=BIG,
        cost_estimate=head_cost(planes * TILE, keys, 16 * devices * TILE * LANES),
        name="shared_head",
    )(place, selected, *owns, *pieces)
    terms = [shift(sent, step + 1) for step, sent in enumerate(outs[2:])]
    rests = pl.pallas_call(
        functools.partial(gather_terms, span),
        in_specs=[VMEM] * (span + 1),
        out_specs=[VMEM] * planes,
        out_shape=[shape(block, LANES)] * planes,
        compiler_params=BIG,
        name="gather_terms",
    )(outs[0], outs[1], *terms)
    rests = spread(rests, span)
    dones = pl.pallas_call(
        functools.partial(whole_head, devices),
        in_specs=[SMEM, SMEM] + [VMEM] * devices,
        out_specs=[VMEM] * devices,
        out_shape=[shape(block, LANES)] * devices,
        scratch_shapes=[
            pltpu.VMEM((devices, TILE, 2 * LANES), jnp.bfloat16),
            pltpu.VMEM((devices, 2 * TILE, LANES), jnp.bfloat16),
        ]
        + head_scratch(devices),
        compiler_params=BIG,
        cost_estimate=head_cost(devices * TILE, keys, 16 * devices * TILE * LANES),
        name="whole_head",
    )(place, selected, *mains[::-1])
    dones = spread(dones, 1)
    wide = shape(height, columns)
    thin = shape(height // POOL, columns, dtype=jnp.float32)
    return pl.pallas_call(
        functools.partial(unpack_body, devices, span),
        in_specs=[SMEM] + [VMEM] * HEADS,
        out_specs=[VMEM] * 6,
        out_shape=[wide, wide, wide, wide, thin, thin],
        compiler_params=BIG,
        name="unpack",
    )(place, *dones[::-1], *rests[::-1])


def shards(query_rows, key_rows, value_rows, out_grad, selected):
    devices = lax.axis_size("ctx")
    planes = HEADS - devices
    tiles_here = query_rows.shape[0] // TILE
    if planes > 0 and devices % planes == 0 and tiles_here == 1 and planes % JOBS == 0:
        span = devices // planes
        if span & (span - 1) == 0:
            return head_shards(query_rows, key_rows, value_rows, out_grad, selected)
    return listed_shards(query_rows, key_rows, value_rows, out_grad, selected)


def solution(mesh):
    in_specs = (
        P(("groups", "ctx"), None),
        P(("groups", "ctx"), None),
        P(("groups", "ctx"), None),
        P(("groups", "ctx"), None),
        P("groups", None),
    )
    out_specs = (
        P(("groups", "ctx"), None),
        P(("groups", "ctx"), None),
        P(("groups", "ctx"), None),
        P(("groups", "ctx"), None),
        P(("groups", "ctx"), None),
        P(("groups", "ctx"), None),
    )
    return jax.shard_map(
        shards, mesh=mesh, in_specs=in_specs, out_specs=out_specs, check_vma=False
    )
```

```python
import functools

import jax
import jax.numpy as jnp
from jax import lax
from jax.experimental import pallas as pl
from jax.experimental.pallas import tpu as pltpu
from jax.sharding import PartitionSpec as P


HEADS = 20
HEAD_DIM = 128
TILE = 128
POOL = 64
SEL = 8


def pooled(rows):
    return jnp.mean(rows.astype(jnp.float32).reshape(-1, POOL, rows.shape[1]), axis=1).astype(
        jnp.bfloat16
    )


def contract(left, right, left_dim, right_dim):
    return lax.dot_general(
        left, right, (((left_dim,), (right_dim,)), ((), ())), preferred_element_type=jnp.float32
    )


def attend(queries, grads_out, keys_all, values_all):
    scaling = HEAD_DIM ** (-0.5)
    out_parts, query_parts, key_parts, value_parts = ([], [], [], [])
    for head in range(HEADS):
        lower = head * HEAD_DIM
        upper = lower + HEAD_DIM
        head_query = queries[:, lower:upper]
        head_grad = grads_out[:, lower:upper]
        head_key = keys_all[:, lower:upper]
        head_value = values_all[:, lower:upper]
        scores = contract(head_query, head_key, 1, 1) * scaling
        summit = jnp.max(scores, axis=-1, keepdims=True)
        raised = jnp.exp(scores - summit)
        weights = raised / jnp.sum(raised, axis=-1, keepdims=True)
        rounded = weights.astype(jnp.bfloat16)
        out_rows = jnp.dot(rounded, head_value, preferred_element_type=jnp.float32).astype(
            jnp.bfloat16
        )
        row_dots = jnp.sum(
            head_grad.astype(jnp.float32) * out_rows.astype(jnp.float32), axis=-1, keepdims=True
        )
        prob_grad = contract(head_grad, head_value, 1, 1)
        score_grad = (weights * (prob_grad - row_dots)).astype(jnp.bfloat16)
        query_grad = jnp.dot(score_grad, head_key, preferred_element_type=jnp.float32) * scaling
        key_terms = contract(score_grad, head_query, 0, 0) * scaling
        value_terms = contract(rounded, head_grad, 0, 0)
        out_parts.append(out_rows)
        query_parts.append(query_grad.astype(jnp.bfloat16))
        key_parts.append(key_terms)
        value_parts.append(value_terms)
    return (
        jnp.concatenate(out_parts, axis=1),
        jnp.concatenate(query_parts, axis=1),
        jnp.concatenate(key_parts, axis=1),
        jnp.concatenate(value_parts, axis=1),
    )


def package(tiles_in, pooled_in, devices, spread):
    tiles_here, tile_len, columns = tiles_in.shape
    per_tile = tile_len // POOL
    split_rows = tiles_in.reshape(tiles_here, devices, spread, columns)
    copies = jnp.broadcast_to(
        pooled_in.reshape(tiles_here, 1, per_tile, columns),
        (tiles_here, devices, per_tile, columns),
    )
    return jnp.concatenate([split_rows, copies], axis=2).reshape(
        tiles_here, devices * (spread + per_tile), columns
    )


def listed_shards(query_rows, key_rows, value_rows, out_grad, selected):
    height, columns = query_rows.shape
    devices = lax.axis_size("ctx")
    tiles_here = height // TILE
    spread = TILE // devices
    own_keys = pooled(key_rows)
    own_values = pooled(value_rows)
    key_tiles = key_rows.reshape(tiles_here, TILE, columns)
    value_tiles = value_rows.reshape(tiles_here, TILE, columns)
    joined_keys, joined_values = (
        lax.all_to_all(
            package(key_tiles, own_keys, devices, spread),
            "ctx",
            split_axis=1,
            concat_axis=0,
            tiled=True,
        ),
        lax.all_to_all(
            package(value_tiles, own_values, devices, spread),
            "ctx",
            split_axis=1,
            concat_axis=0,
            tiled=True,
        ),
    )
    held_keys = joined_keys[:, :spread]
    held_values = joined_values[:, :spread]
    pool_keys = joined_keys[:, spread:].reshape(-1, columns)
    pool_values = joined_values[:, spread:].reshape(-1, columns)
    comp_count = pool_keys.shape[0]
    got_keys, got_values = (
        lax.all_to_all(held_keys[selected], "ctx", split_axis=0, concat_axis=2, tiled=True),
        lax.all_to_all(held_values[selected], "ctx", split_axis=0, concat_axis=2, tiled=True),
    )
    fine_keys = got_keys.reshape(tiles_here, SEL * TILE, columns)
    fine_values = got_values.reshape(tiles_here, SEL * TILE, columns)
    out_tiles, query_tiles, key_listed, value_listed = ([], [], [], [])
    keys_all = jnp.concatenate([pool_keys, fine_keys[0]], axis=0)
    values_all = jnp.concatenate([pool_values, fine_values[0]], axis=0)
    out_rows, query_grad, key_terms, value_terms = attend(
        query_rows, out_grad, keys_all, values_all
    )
    out_tiles.append(out_rows)
    query_tiles.append(query_grad)
    coarse_keys = key_terms[:comp_count]
    coarse_values = value_terms[:comp_count]
    key_listed.append(key_terms[comp_count:].astype(jnp.bfloat16))
    value_listed.append(value_terms[comp_count:].astype(jnp.bfloat16))
    own_coarse_keys, own_coarse_values = (
        lax.psum_scatter(coarse_keys, "ctx", scatter_dimension=0, tiled=True),
        lax.psum_scatter(coarse_values, "ctx", scatter_dimension=0, tiled=True),
    )
    listed_keys = jnp.stack(key_listed).reshape(tiles_here * SEL, devices, spread, columns)
    listed_values = jnp.stack(value_listed).reshape(tiles_here * SEL, devices, spread, columns)
    back_keys, back_values = (
        lax.all_to_all(listed_keys, "ctx", split_axis=1, concat_axis=0, tiled=True),
        lax.all_to_all(listed_values, "ctx", split_axis=1, concat_axis=0, tiled=True),
    )
    tile_ids = jnp.arange(selected.shape[0], dtype=jnp.int32)[:, None]
    member = (selected.reshape(1, -1) == tile_ids).astype(jnp.bfloat16)
    entries = member.shape[1]
    sum_keys = jnp.dot(
        member, back_keys.reshape(entries, spread * columns), preferred_element_type=jnp.float32
    )
    sum_values = jnp.dot(
        member, back_values.reshape(entries, spread * columns), preferred_element_type=jnp.float32
    )
    held_key_grad = sum_keys.astype(jnp.bfloat16).reshape(devices, tiles_here, spread, columns)
    held_value_grad = sum_values.astype(jnp.bfloat16).reshape(devices, tiles_here, spread, columns)
    owned_keys, owned_values = (
        lax.all_to_all(held_key_grad, "ctx", split_axis=0, concat_axis=2, tiled=True),
        lax.all_to_all(held_value_grad, "ctx", split_axis=0, concat_axis=2, tiled=True),
    )
    grad_key = (
        owned_keys.reshape(height, columns).astype(jnp.float32)
        + jnp.repeat(own_coarse_keys, POOL, axis=0) / POOL
    ).astype(jnp.bfloat16)
    grad_value = (
        owned_values.reshape(height, columns).astype(jnp.float32)
        + jnp.repeat(own_coarse_values, POOL, axis=0) / POOL
    ).astype(jnp.bfloat16)
    attended = out_tiles[0]
    grad_query = query_tiles[0]
    return (attended, grad_query, grad_key, grad_value, own_coarse_keys, own_coarse_values)


LANES = 128
JOBS = 4
SPLITS = 2
VMEM = pl.BlockSpec(memory_space=pltpu.VMEM)
SMEM = pl.BlockSpec(memory_space=pltpu.SMEM)
BIG = pltpu.CompilerParams(vmem_limit_bytes=50 * 1024 * 1024)


def nt(left, right):
    return contract(left, right, 1, 1)


def nn(left, right):
    return contract(left, right, 1, 0)


def split_rows(total):
    parts = []
    for _ in range(SPLITS):
        part = total.astype(jnp.bfloat16)
        parts.append(part.astype(jnp.float32))
        total = total - parts[-1]
    return parts


def tail_rows(coarse_key, coarse_value):
    per_tile = TILE // POOL
    parts = split_rows(jnp.concatenate([coarse_key, coarse_value], axis=0))
    used = SPLITS * 2 * per_tile
    if used < tail_height():
        parts.append(jnp.zeros((tail_height() - used, LANES), jnp.float32))
    return jnp.concatenate(parts, axis=0).astype(jnp.bfloat16)


def tail_height():
    used = SPLITS * 2 * (TILE // POOL)
    return -(-used // 8) * 8


def join_tail(tail):
    pair = 2 * (TILE // POOL)
    rows = tail.astype(jnp.float32)
    total = rows[:pair]
    for part in range(1, SPLITS):
        total = total + rows[part * pair : (part + 1) * pair]
    return total


def lane_block(index):
    return pl.ds(pl.multiple_of(index * LANES, LANES), LANES)


def pack_body(first, place_ref, q_ref, k_ref, v_ref, g_ref, *out_refs):
    for step, out_ref in enumerate(out_refs):
        columns = lane_block(first + lax.bitwise_xor(place_ref[0], step))
        for index, ref in enumerate((q_ref, k_ref, v_ref, g_ref)):
            out_ref[index * TILE : (index + 1) * TILE, :] = ref[:, columns]


def pack(arrays, place, first, count):
    width = arrays[0].shape[1]
    if first % count == 0:
        spec = pl.BlockSpec((TILE, count * LANES), lambda i, _: (0, first // count))
        start = 0
    else:
        spec = pl.BlockSpec((TILE, width), lambda i, _: (0, 0))
        start = first
    out = pl.BlockSpec((4 * TILE, LANES), lambda i, _: (0, 0))
    return pl.pallas_call(
        functools.partial(pack_body, start),
        grid_spec=pltpu.PrefetchScalarGridSpec(
            num_scalar_prefetch=1, grid=(1,), in_specs=[spec] * 4, out_specs=[out] * count
        ),
        out_shape=[jax.ShapeDtypeStruct((4 * TILE, LANES), jnp.bfloat16)] * count,
        cost_estimate=pl.CostEstimate(
            flops=0, transcendentals=0, bytes_accessed=16 * count * TILE * LANES
        ),
        name="pack",
    )(place, *arrays)


def prepare(scratch):
    rows_ref, pool_key, pool_value, key_t, value_t, both_sum, pool_key_sum, pool_value_sum = scratch
    per_tile = TILE // POOL

    def one(tile, carry):
        for place, pool_ref, flip_ref in ((0, pool_key, key_t), (1, pool_value, value_t)):
            rows = rows_ref[tile, :, place * LANES : (place + 1) * LANES].astype(jnp.float32)
            means = [
                jnp.mean(rows[part * POOL : (part + 1) * POOL], axis=0, keepdims=True)
                for part in range(per_tile)
            ]
            pool_ref[pl.ds(tile * per_tile, per_tile), :] = jnp.concatenate(means, axis=0)
            flip_ref[tile] = rows.T.astype(jnp.bfloat16)
        both_sum[tile] = jnp.zeros((TILE, 2 * LANES), jnp.float32)
        return carry

    lax.fori_loop(0, rows_ref.shape[0], one, 0)
    pool_key_sum[...] = jnp.zeros_like(pool_key_sum)
    pool_value_sum[...] = jnp.zeros_like(pool_value_sum)


def wide_pair(left, right):
    zeros = jnp.zeros_like(left)
    return jnp.concatenate(
        [jnp.concatenate([left, zeros], axis=1), jnp.concatenate([zeros, right], axis=1)], axis=0
    )


def some_tiles(jobs, scratch, work):
    rows_ref, pool_key, pool_value, key_t, value_t, both_sum, pool_key_sum, pool_value_sum = scratch
    scaling = HEAD_DIM ** (-0.5)
    base2 = scaling * 1.4426950408889634
    comp = pool_key.shape[0]
    coarse_key = pool_key[...].astype(jnp.bfloat16)
    coarse_value = pool_value[...].astype(jnp.bfloat16)
    coarse = jnp.concatenate([coarse_key, coarse_value], axis=1)
    fine = SEL * TILE
    spans = [(slot * TILE, TILE) for slot in range(SEL)] + [(fine, comp)]
    results = []
    for (query, grad, listed), (score_ref, prob_ref, pair_ref) in zip(jobs, work):
        pair = wide_pair(query, grad)
        rows = [rows_ref[tile] for tile in listed]
        both = nt(jnp.concatenate(rows + [coarse], axis=0), pair)
        score_ref[...] = both[:, :LANES]
        prob_ref[...] = both[:, LANES:]
        top = jnp.max(both[:, :LANES], axis=0, keepdims=True)
        results.append((pair, top))
    for index, (_, (score_ref, prob_ref, pair_ref)) in enumerate(zip(jobs, work)):
        pair, top = results[index]
        raised = jnp.exp2((score_ref[...] - top) * base2)
        score_ref[...] = raised
        inverse = 1.0 / jnp.sum(raised, axis=0, keepdims=True)
        results[index] = (pair, inverse)
    outs = []
    for index, ((query, grad, listed), (score_ref, prob_ref, pair_ref)) in enumerate(zip(jobs, work)):
        pair, inverse = results[index]
        weight = score_ref[...] * inverse
        rounded = weight.astype(jnp.bfloat16)
        pair_ref[:, LANES:] = rounded
        score_ref[...] = weight
        values_t = jnp.concatenate([value_t[tile] for tile in listed], axis=1)
        out_t = nn(values_t, pair_ref[:fine, LANES:]) + contract(
            coarse_value, pair_ref[fine:, LANES:], 0, 0
        )
        out_t = out_t.astype(jnp.bfloat16).astype(jnp.float32)
        dots = jnp.sum(out_t * grad.astype(jnp.float32).T, axis=0, keepdims=True)
        outs.append((out_t, dots))
    for index, ((query, grad, listed), (score_ref, prob_ref, pair_ref)) in enumerate(zip(jobs, work)):
        out_t, dots = outs[index]
        slope = (score_ref[...] * (prob_ref[...] - dots)).astype(jnp.bfloat16)
        pair_ref[:, :LANES] = slope
        terms = nn(pair_ref[...], results[index][0])
        for tile, (start, size) in zip(listed, spans):
            both_sum[tile] += terms[start : start + size]
        pool_key_sum[...] += terms[fine:, :LANES]
        pool_value_sum[...] += terms[fine:, LANES:]
        keys_t = jnp.concatenate([key_t[tile] for tile in listed], axis=1)
        query_t = nn(keys_t, pair_ref[:fine, :LANES]) + contract(
            coarse_key, pair_ref[fine:, :LANES], 0, 0
        )
        outs[index] = (
            out_t.T.astype(jnp.bfloat16),
            (query_t.T * scaling).astype(jnp.bfloat16),
        )
    return outs


def finish(tile, scratch):
    scaling = HEAD_DIM ** (-0.5)
    both_sum, pool_key_sum, pool_value_sum = scratch
    per_tile = TILE // POOL
    coarse_key = pool_key_sum[pl.ds(tile * per_tile, per_tile), :] * scaling
    coarse_value = pool_value_sum[pl.ds(tile * per_tile, per_tile), :]

    def whole(fine, coarse):
        return jnp.concatenate(
            [
                fine[part * POOL : (part + 1) * POOL] + coarse[part : part + 1] * (1.0 / POOL)
                for part in range(per_tile)
            ],
            axis=0,
        )

    return (
        whole(both_sum[tile, :, :LANES] * scaling, coarse_key),
        whole(both_sum[tile, :, LANES:], coarse_value),
        coarse_key,
        coarse_value,
    )


def head_scratch(tiles):
    comp = tiles * (TILE // POOL)
    keys = SEL * TILE + comp
    return [
        pltpu.VMEM((tiles, TILE, 2 * LANES), jnp.bfloat16),
        pltpu.VMEM((comp, LANES), jnp.float32),
        pltpu.VMEM((comp, LANES), jnp.float32),
        pltpu.VMEM((tiles, LANES, TILE), jnp.bfloat16),
        pltpu.VMEM((tiles, LANES, TILE), jnp.bfloat16),
        pltpu.VMEM((tiles, TILE, 2 * LANES), jnp.float32),
        pltpu.VMEM((comp, LANES), jnp.float32),
        pltpu.VMEM((comp, LANES), jnp.float32),
    ] + JOBS * [
        pltpu.VMEM((keys, LANES), jnp.float32),
        pltpu.VMEM((keys, LANES), jnp.float32),
        pltpu.VMEM((keys, 2 * LANES), jnp.bfloat16),
    ]


def split_scratch(scratch):
    totals, work = scratch[:8], scratch[8:]
    return totals, [work[3 * job : 3 * job + 3] for job in range(JOBS)]


def head_cost(queries, keys, moved):
    return pl.CostEstimate(
        flops=12 * queries * keys * LANES,
        transcendentals=queries * keys,
        bytes_accessed=moved,
    )


def every_tile(count, stride, place_ref, sel_ref, query_ref, out_ref, totals, work):
    place = place_ref[0]

    def some(first, carry):
        jobs = []
        for job in range(JOBS):
            piece = first * JOBS + job
            tile = lax.bitwise_xor(place, piece * stride)
            listed = [lax.bitwise_xor(sel_ref[tile, slot], place) for slot in range(SEL)]
            jobs.append((query_ref[piece, :, :LANES], query_ref[piece, :, LANES:], listed))
        for job, (rows, slopes) in enumerate(some_tiles(jobs, totals, work)):
            out_ref[first * JOBS + job, :TILE, :] = rows
            out_ref[first * JOBS + job, TILE : 2 * TILE, :] = slopes
        return carry

    lax.fori_loop(0, count // JOBS, some, 0)


def whole_head(tiles, place_ref, sel_ref, *refs):
    pieces, outs = refs[:tiles][::-1], refs[tiles : 2 * tiles]
    query_ref, out_ref = refs[2 * tiles : 2 * tiles + 2]
    totals, work = split_scratch(refs[2 * tiles + 2 :])
    for step, piece in enumerate(pieces):
        query_ref[step, :, :LANES] = piece[:TILE, :]
        totals[0][step, :, :LANES] = piece[TILE : 2 * TILE, :]
        totals[0][step, :, LANES:] = piece[2 * TILE : 3 * TILE, :]
        query_ref[step, :, LANES:] = piece[3 * TILE :, :]
    prepare(totals)
    every_tile(tiles, 1, place_ref, sel_ref, query_ref, out_ref, totals, work)
    for step, out in enumerate(outs):
        key, value, coarse_key, coarse_value = finish(step, totals[5:])
        out[: 2 * TILE, :] = out_ref[step]
        out[2 * TILE : 3 * TILE, :] = key.astype(jnp.bfloat16)
        out[3 * TILE : 4 * TILE, :] = value.astype(jnp.bfloat16)
        out[4 * TILE :, :] = tail_rows(coarse_key, coarse_value)


def shared_head(span, planes, place_ref, sel_ref, *refs):
    owns, refs = refs[:planes], refs[planes:]
    pieces, refs = refs[: span - 1], refs[span - 1 :]
    out_ref, keep_ref, send_ref, query_ref = refs[:4]
    totals, work = split_scratch(refs[4:])
    for plane, own in enumerate(owns):
        query_ref[plane, :, :LANES] = own[:TILE, :]
        query_ref[plane, :, LANES:] = own[3 * TILE :, :]
        totals[0][plane * span, :, :LANES] = own[TILE : 2 * TILE, :]
        totals[0][plane * span, :, LANES:] = own[2 * TILE : 3 * TILE, :]
        for step in range(1, span):
            piece = pieces[step - 1]
            totals[0][plane * span + step, :, :LANES] = piece[plane, :TILE, :]
            totals[0][plane * span + step, :, LANES:] = piece[plane, TILE:, :]
    prepare(totals)
    every_tile(planes, span, place_ref, sel_ref, query_ref, out_ref, totals, work)
    for step in range(span):

        def last(plane, carry, step=step):
            terms = finish(plane * span + step, totals[5:])
            if step % 2 == 0:
                keep_terms(keep_ref, step // 2, plane, *terms)
            else:
                send_terms(send_ref, step // 2, plane, *terms)
            return carry

        lax.fori_loop(0, planes, last, 0)


def keep_terms(ref, index, plane, key, value, coarse_key, coarse_value):
    rows = [coarse_key, coarse_value]
    filler = 8 - 2 * (TILE // POOL)
    if filler:
        rows.append(jnp.zeros((filler, LANES), jnp.float32))
    ref[index, plane, :TILE, :] = key
    ref[index, plane, TILE : 2 * TILE, :] = value
    ref[index, plane, 2 * TILE :, :] = jnp.concatenate(rows, axis=0)


def send_terms(ref, index, plane, key, value, coarse_key, coarse_value):
    ref[index, plane, :TILE, :] = key.astype(jnp.bfloat16)
    ref[index, plane, TILE : 2 * TILE, :] = value.astype(jnp.bfloat16)
    ref[index, plane, 2 * TILE :, :] = tail_rows(coarse_key, coarse_value)


def add_terms(keep_ref, piece_ref, index, plane):
    per_tile = TILE // POOL
    fine = keep_ref[index, plane, : 2 * TILE, :]
    fine = fine + piece_ref[index, plane, : 2 * TILE, :].astype(jnp.float32)
    coarse = keep_ref[index, plane, 2 * TILE : 2 * TILE + 2 * per_tile, :]
    coarse = coarse + join_tail(piece_ref[index, plane, 2 * TILE :, :])
    return fine[:TILE], fine[TILE:], coarse[:per_tile], coarse[per_tile:]


def fold_terms(count, planes, keep_ref, piece_ref, next_ref, send_ref):
    for index in range(count):
        for plane in range(planes):
            terms = add_terms(keep_ref, piece_ref, index, plane)
            if index % 2 == 0:
                keep_terms(next_ref, index // 2, plane, *terms)
            else:
                send_terms(send_ref, index // 2, plane, *terms)


def last_terms(rows_ref, keep_ref, piece_ref, *outs):
    for plane, out in enumerate(outs):
        key, value, coarse_key, coarse_value = add_terms(keep_ref, piece_ref, 0, plane)
        out[: 2 * TILE, :] = rows_ref[plane]
        out[2 * TILE : 3 * TILE, :] = key.astype(jnp.bfloat16)
        out[3 * TILE : 4 * TILE, :] = value.astype(jnp.bfloat16)
        out[4 * TILE :, :] = tail_rows(coarse_key, coarse_value)


def unpack_body(heads, span, place_ref, *refs):
    pieces, (a_ref, q_ref, k_ref, v_ref, pk_ref, pv_ref) = refs[:-6], refs[-6:]
    pieces = pieces[:heads][::-1] + pieces[heads:][::-1]
    per_tile = TILE // POOL
    place = place_ref[0]
    for step, ref in enumerate(pieces):
        if step < heads:
            head = lax.bitwise_xor(place, step)
        else:
            head = heads + lax.bitwise_xor(place // span, step - heads)
        columns = lane_block(head)
        for index, out in enumerate((a_ref, q_ref, k_ref, v_ref)):
            out[:, columns] = ref[index * TILE : (index + 1) * TILE, :]
        coarse = join_tail(ref[4 * TILE :, :])
        pk_ref[:, columns] = coarse[:per_tile]
        pv_ref[:, columns] = coarse[per_tile:]


def head_shards(query_rows, key_rows, value_rows, out_grad, selected):
    devices = lax.axis_size("ctx")
    height, columns = query_rows.shape
    planes = HEADS - devices
    span = devices // planes
    arrays = (query_rows, key_rows, value_rows, out_grad)
    place = jnp.reshape(lax.axis_index("ctx"), (1,))

    def shift(block, step):
        return lax.ppermute(block, "ctx", [(i, i ^ step) for i in range(devices)])

    def spread(pieces, stride):
        moved = [pieces[0]]
        for step in range(1, len(pieces)):
            moved.append(shift(pieces[step], step * stride))
        return moved

    def shape(*dims, dtype=jnp.bfloat16):
        return jax.ShapeDtypeStruct(dims, dtype)

    block = 4 * TILE + tail_height()
    part = 2 * TILE + tail_height()
    keys = SEL * TILE + devices * (TILE // POOL)
    owns = spread(pack(arrays, place // span, devices, planes), span)
    mains = spread(pack(arrays, place, 0, devices), 1)
    own_kv = jnp.stack([own[TILE : 3 * TILE] for own in owns])
    pieces = {0: own_kv}
    hops = [1 << bit for bit in reversed(range(span.bit_length() - 1))]
    for hop in hops:
        held = sorted(pieces)
        for step in held:
            pieces[step ^ hop] = shift(pieces[step], hop)
    pieces = [pieces[step] for step in range(1, span)]
    half = span // 2
    rows, keep, send = pl.pallas_call(
        functools.partial(shared_head, span, planes),
        in_specs=[SMEM, SMEM] + [VMEM] * (planes + span - 1),
        out_specs=[VMEM] * 3,
        out_shape=[
            shape(planes, 2 * TILE, LANES),
            shape(half, planes, 2 * TILE + 8, LANES, dtype=jnp.float32),
            shape(half, planes, part, LANES),
        ],
        scratch_shapes=[pltpu.VMEM((planes, TILE, 2 * LANES), jnp.bfloat16)]
        + head_scratch(devices),
        compiler_params=BIG,
        cost_estimate=head_cost(planes * TILE, keys, 16 * devices * TILE * LANES),
        name="shared_head",
    )(place, selected, *owns, *pieces)
    hop = 1
    while half > 1:
        got = shift(send, hop)
        keep, send = pl.pallas_call(
            functools.partial(fold_terms, half, planes),
            in_specs=[VMEM] * 2,
            out_specs=[VMEM] * 2,
            out_shape=[
                shape(half // 2, planes, 2 * TILE + 8, LANES, dtype=jnp.float32),
                shape(half // 2, planes, part, LANES),
            ],
            compiler_params=BIG,
            name="fold_terms",
        )(keep, got)
        half, hop = half // 2, hop * 2
    got = shift(send, hop)
    rests = pl.pallas_call(
        last_terms,
        in_specs=[VMEM] * 3,
        out_specs=[VMEM] * planes,
        out_shape=[shape(block, LANES)] * planes,
        compiler_params=BIG,
        name="last_terms",
    )(rows, keep, got)
    rests = spread(rests, span)
    dones = pl.pallas_call(
        functools.partial(whole_head, devices),
        in_specs=[SMEM, SMEM] + [VMEM] * devices,
        out_specs=[VMEM] * devices,
        out_shape=[shape(block, LANES)] * devices,
        scratch_shapes=[
            pltpu.VMEM((devices, TILE, 2 * LANES), jnp.bfloat16),
            pltpu.VMEM((devices, 2 * TILE, LANES), jnp.bfloat16),
        ]
        + head_scratch(devices),
        compiler_params=BIG,
        cost_estimate=head_cost(devices * TILE, keys, 16 * devices * TILE * LANES),
        name="whole_head",
    )(place, selected, *mains[::-1])
    dones = spread(dones, 1)
    wide = shape(height, columns)
    thin = shape(height // POOL, columns, dtype=jnp.float32)
    return pl.pallas_call(
        functools.partial(unpack_body, devices, span),
        in_specs=[SMEM] + [VMEM] * HEADS,
        out_specs=[VMEM] * 6,
        out_shape=[wide, wide, wide, wide, thin, thin],
        compiler_params=BIG,
        name="unpack",
    )(place, *dones[::-1], *rests[::-1])


def shards(query_rows, key_rows, value_rows, out_grad, selected):
    devices = lax.axis_size("ctx")
    planes = HEADS - devices
    tiles_here = query_rows.shape[0] // TILE
    if planes > 0 and devices % planes == 0 and tiles_here == 1 and planes % JOBS == 0:
        span = devices // planes
        if span & (span - 1) == 0:
            return head_shards(query_rows, key_rows, value_rows, out_grad, selected)
    return listed_shards(query_rows, key_rows, value_rows, out_grad, selected)


def solution(mesh):
    in_specs = (
        P(("groups", "ctx"), None),
        P(("groups", "ctx"), None),
        P(("groups", "ctx"), None),
        P(("groups", "ctx"), None),
        P("groups", None),
    )
    out_specs = (
        P(("groups", "ctx"), None),
        P(("groups", "ctx"), None),
        P(("groups", "ctx"), None),
        P(("groups", "ctx"), None),
        P(("groups", "ctx"), None),
        P(("groups", "ctx"), None),
    )
    return jax.shard_map(
        shards, mesh=mesh, in_specs=in_specs, out_specs=out_specs, check_vma=False
    )
```

```python
import functools

import jax
import jax.numpy as jnp
from jax import lax
from jax.experimental import pallas as pl
from jax.experimental.pallas import tpu as pltpu
from jax.sharding import PartitionSpec as P


HEADS = 20
HEAD_DIM = 128
TILE = 128
POOL = 64
SEL = 8


def pooled(rows):
    return jnp.mean(rows.astype(jnp.float32).reshape(-1, POOL, rows.shape[1]), axis=1).astype(
        jnp.bfloat16
    )


def contract(left, right, left_dim, right_dim):
    return lax.dot_general(
        left, right, (((left_dim,), (right_dim,)), ((), ())), preferred_element_type=jnp.float32
    )


def attend(queries, grads_out, keys_all, values_all):
    scaling = HEAD_DIM ** (-0.5)
    out_parts, query_parts, key_parts, value_parts = ([], [], [], [])
    for head in range(HEADS):
        lower = head * HEAD_DIM
        upper = lower + HEAD_DIM
        head_query = queries[:, lower:upper]
        head_grad = grads_out[:, lower:upper]
        head_key = keys_all[:, lower:upper]
        head_value = values_all[:, lower:upper]
        scores = contract(head_query, head_key, 1, 1) * scaling
        summit = jnp.max(scores, axis=-1, keepdims=True)
        raised = jnp.exp(scores - summit)
        weights = raised / jnp.sum(raised, axis=-1, keepdims=True)
        rounded = weights.astype(jnp.bfloat16)
        out_rows = jnp.dot(rounded, head_value, preferred_element_type=jnp.float32).astype(
            jnp.bfloat16
        )
        row_dots = jnp.sum(
            head_grad.astype(jnp.float32) * out_rows.astype(jnp.float32), axis=-1, keepdims=True
        )
        prob_grad = contract(head_grad, head_value, 1, 1)
        score_grad = (weights * (prob_grad - row_dots)).astype(jnp.bfloat16)
        query_grad = jnp.dot(score_grad, head_key, preferred_element_type=jnp.float32) * scaling
        key_terms = contract(score_grad, head_query, 0, 0) * scaling
        value_terms = contract(rounded, head_grad, 0, 0)
        out_parts.append(out_rows)
        query_parts.append(query_grad.astype(jnp.bfloat16))
        key_parts.append(key_terms)
        value_parts.append(value_terms)
    return (
        jnp.concatenate(out_parts, axis=1),
        jnp.concatenate(query_parts, axis=1),
        jnp.concatenate(key_parts, axis=1),
        jnp.concatenate(value_parts, axis=1),
    )


def package(tiles_in, pooled_in, devices, spread):
    tiles_here, tile_len, columns = tiles_in.shape
    per_tile = tile_len // POOL
    split_rows = tiles_in.reshape(tiles_here, devices, spread, columns)
    copies = jnp.broadcast_to(
        pooled_in.reshape(tiles_here, 1, per_tile, columns),
        (tiles_here, devices, per_tile, columns),
    )
    return jnp.concatenate([split_rows, copies], axis=2).reshape(
        tiles_here, devices * (spread + per_tile), columns
    )


def listed_shards(query_rows, key_rows, value_rows, out_grad, selected):
    height, columns = query_rows.shape
    devices = lax.axis_size("ctx")
    tiles_here = height // TILE
    spread = TILE // devices
    own_keys = pooled(key_rows)
    own_values = pooled(value_rows)
    key_tiles = key_rows.reshape(tiles_here, TILE, columns)
    value_tiles = value_rows.reshape(tiles_here, TILE, columns)
    joined_keys, joined_values = (
        lax.all_to_all(
            package(key_tiles, own_keys, devices, spread),
            "ctx",
            split_axis=1,
            concat_axis=0,
            tiled=True,
        ),
        lax.all_to_all(
            package(value_tiles, own_values, devices, spread),
            "ctx",
            split_axis=1,
            concat_axis=0,
            tiled=True,
        ),
    )
    held_keys = joined_keys[:, :spread]
    held_values = joined_values[:, :spread]
    pool_keys = joined_keys[:, spread:].reshape(-1, columns)
    pool_values = joined_values[:, spread:].reshape(-1, columns)
    comp_count = pool_keys.shape[0]
    got_keys, got_values = (
        lax.all_to_all(held_keys[selected], "ctx", split_axis=0, concat_axis=2, tiled=True),
        lax.all_to_all(held_values[selected], "ctx", split_axis=0, concat_axis=2, tiled=True),
    )
    fine_keys = got_keys.reshape(tiles_here, SEL * TILE, columns)
    fine_values = got_values.reshape(tiles_here, SEL * TILE, columns)
    out_tiles, query_tiles, key_listed, value_listed = ([], [], [], [])
    keys_all = jnp.concatenate([pool_keys, fine_keys[0]], axis=0)
    values_all = jnp.concatenate([pool_values, fine_values[0]], axis=0)
    out_rows, query_grad, key_terms, value_terms = attend(
        query_rows, out_grad, keys_all, values_all
    )
    out_tiles.append(out_rows)
    query_tiles.append(query_grad)
    coarse_keys = key_terms[:comp_count]
    coarse_values = value_terms[:comp_count]
    key_listed.append(key_terms[comp_count:].astype(jnp.bfloat16))
    value_listed.append(value_terms[comp_count:].astype(jnp.bfloat16))
    own_coarse_keys, own_coarse_values = (
        lax.psum_scatter(coarse_keys, "ctx", scatter_dimension=0, tiled=True),
        lax.psum_scatter(coarse_values, "ctx", scatter_dimension=0, tiled=True),
    )
    listed_keys = jnp.stack(key_listed).reshape(tiles_here * SEL, devices, spread, columns)
    listed_values = jnp.stack(value_listed).reshape(tiles_here * SEL, devices, spread, columns)
    back_keys, back_values = (
        lax.all_to_all(listed_keys, "ctx", split_axis=1, concat_axis=0, tiled=True),
        lax.all_to_all(listed_values, "ctx", split_axis=1, concat_axis=0, tiled=True),
    )
    tile_ids = jnp.arange(selected.shape[0], dtype=jnp.int32)[:, None]
    member = (selected.reshape(1, -1) == tile_ids).astype(jnp.bfloat16)
    entries = member.shape[1]
    sum_keys = jnp.dot(
        member, back_keys.reshape(entries, spread * columns), preferred_element_type=jnp.float32
    )
    sum_values = jnp.dot(
        member, back_values.reshape(entries, spread * columns), preferred_element_type=jnp.float32
    )
    held_key_grad = sum_keys.astype(jnp.bfloat16).reshape(devices, tiles_here, spread, columns)
    held_value_grad = sum_values.astype(jnp.bfloat16).reshape(devices, tiles_here, spread, columns)
    owned_keys, owned_values = (
        lax.all_to_all(held_key_grad, "ctx", split_axis=0, concat_axis=2, tiled=True),
        lax.all_to_all(held_value_grad, "ctx", split_axis=0, concat_axis=2, tiled=True),
    )
    grad_key = (
        owned_keys.reshape(height, columns).astype(jnp.float32)
        + jnp.repeat(own_coarse_keys, POOL, axis=0) / POOL
    ).astype(jnp.bfloat16)
    grad_value = (
        owned_values.reshape(height, columns).astype(jnp.float32)
        + jnp.repeat(own_coarse_values, POOL, axis=0) / POOL
    ).astype(jnp.bfloat16)
    attended = out_tiles[0]
    grad_query = query_tiles[0]
    return (attended, grad_query, grad_key, grad_value, own_coarse_keys, own_coarse_values)


LANES = 128
JOBS = (8, 4, 2, 1)
SPLITS = 2
VMEM = pl.BlockSpec(memory_space=pltpu.VMEM)
SMEM = pl.BlockSpec(memory_space=pltpu.SMEM)
BIG = pltpu.CompilerParams(vmem_limit_bytes=50 * 1024 * 1024)


def nt(left, right):
    return contract(left, right, 1, 1)


def nn(left, right):
    return contract(left, right, 1, 0)


def split_rows(total):
    parts = []
    for _ in range(SPLITS):
        part = total.astype(jnp.bfloat16)
        parts.append(part.astype(jnp.float32))
        total = total - parts[-1]
    return parts


def tail_rows(coarse_key, coarse_value):
    per_tile = TILE // POOL
    parts = split_rows(jnp.concatenate([coarse_key, coarse_value], axis=0))
    used = SPLITS * 2 * per_tile
    if used < tail_height():
        parts.append(jnp.zeros((tail_height() - used, LANES), jnp.float32))
    return jnp.concatenate(parts, axis=0).astype(jnp.bfloat16)


def tail_height():
    used = SPLITS * 2 * (TILE // POOL)
    return -(-used // 8) * 8


def join_tail(tail):
    pair = 2 * (TILE // POOL)
    rows = tail.astype(jnp.float32)
    total = rows[:pair]
    for part in range(1, SPLITS):
        total = total + rows[part * pair : (part + 1) * pair]
    return total


def lane_block(index):
    return pl.ds(pl.multiple_of(index * LANES, LANES), LANES)


def pack_body(first, place_ref, q_ref, k_ref, v_ref, g_ref, *out_refs):
    for step, out_ref in enumerate(out_refs):
        columns = lane_block(first + lax.bitwise_xor(place_ref[0], step))
        for index, ref in enumerate((q_ref, k_ref, v_ref, g_ref)):
            out_ref[index * TILE : (index + 1) * TILE, :] = ref[:, columns]


def pack(arrays, place, first, count):
    width = arrays[0].shape[1]
    if first % count == 0:
        spec = pl.BlockSpec((TILE, count * LANES), lambda i, _: (0, first // count))
        start = 0
    else:
        spec = pl.BlockSpec((TILE, width), lambda i, _: (0, 0))
        start = first
    out = pl.BlockSpec((4 * TILE, LANES), lambda i, _: (0, 0))
    return pl.pallas_call(
        functools.partial(pack_body, start),
        grid_spec=pltpu.PrefetchScalarGridSpec(
            num_scalar_prefetch=1, grid=(1,), in_specs=[spec] * 4, out_specs=[out] * count
        ),
        out_shape=[jax.ShapeDtypeStruct((4 * TILE, LANES), jnp.bfloat16)] * count,
        cost_estimate=pl.CostEstimate(
            flops=0, transcendentals=0, bytes_accessed=16 * count * TILE * LANES
        ),
        name="pack",
    )(place, *arrays)


def prepare(scratch):
    rows_ref, pool_key, pool_value, key_t, value_t, both_sum, pool_key_sum, pool_value_sum = scratch
    per_tile = TILE // POOL

    def one(tile, carry):
        for place, pool_ref, flip_ref in ((0, pool_key, key_t), (1, pool_value, value_t)):
            rows = rows_ref[tile, :, place * LANES : (place + 1) * LANES].astype(jnp.float32)
            means = [
                jnp.mean(rows[part * POOL : (part + 1) * POOL], axis=0, keepdims=True)
                for part in range(per_tile)
            ]
            pool_ref[pl.ds(tile * per_tile, per_tile), :] = jnp.concatenate(means, axis=0)
            flip_ref[tile] = rows.T.astype(jnp.bfloat16)
        both_sum[tile] = jnp.zeros((TILE, 2 * LANES), jnp.float32)
        return carry

    lax.fori_loop(0, rows_ref.shape[0], one, 0)
    pool_key_sum[...] = jnp.zeros_like(pool_key_sum)
    pool_value_sum[...] = jnp.zeros_like(pool_value_sum)


def wide_pair(left, right):
    zeros = jnp.zeros_like(left)
    return jnp.concatenate(
        [jnp.concatenate([left, zeros], axis=1), jnp.concatenate([zeros, right], axis=1)], axis=0
    )


def some_tiles(jobs, scratch, work):
    rows_ref, pool_key, pool_value, key_t, value_t, both_sum, pool_key_sum, pool_value_sum = scratch
    scaling = HEAD_DIM ** (-0.5)
    base2 = scaling * 1.4426950408889634
    comp = pool_key.shape[0]
    coarse_key = pool_key[...].astype(jnp.bfloat16)
    coarse_value = pool_value[...].astype(jnp.bfloat16)
    coarse = jnp.concatenate([coarse_key, coarse_value], axis=1)
    fine = SEL * TILE
    spans = [(slot * TILE, TILE) for slot in range(SEL)] + [(fine, comp)]
    results = []
    for (query, grad, listed), (score_ref, prob_ref, pair_ref) in zip(jobs, work):
        pair = wide_pair(query, grad)
        rows = [rows_ref[tile] for tile in listed]
        both = nt(jnp.concatenate(rows + [coarse], axis=0), pair)
        score_ref[...] = both[:, :LANES]
        prob_ref[...] = both[:, LANES:]
        top = jnp.max(both[:, :LANES], axis=0, keepdims=True)
        results.append((pair, top))
    for index, (_, (score_ref, prob_ref, pair_ref)) in enumerate(zip(jobs, work)):
        pair, top = results[index]
        total = jnp.zeros((8, LANES), jnp.float32)
        for start, size in spans:
            raised = jnp.exp2((score_ref[start : start + size] - top) * base2)
            score_ref[start : start + size] = raised
            total = total + jnp.sum(raised.reshape(size // 8, 8, LANES), axis=0)
        inverse = 1.0 / jnp.sum(total, axis=0, keepdims=True)
        results[index] = (pair, inverse)
    outs = []
    for index, ((query, grad, listed), (score_ref, prob_ref, pair_ref)) in enumerate(zip(jobs, work)):
        pair, inverse = results[index]
        for start, size in spans:
            weight = score_ref[start : start + size] * inverse
            pair_ref[start : start + size, LANES:] = weight.astype(jnp.bfloat16)
            score_ref[start : start + size] = weight
        out_t = contract(coarse_value, pair_ref[fine:, LANES:], 0, 0)
        for slot in range(0, SEL, 2):
            values_t = jnp.concatenate([value_t[tile] for tile in listed[slot : slot + 2]], axis=1)
            out_t = out_t + nn(values_t, pair_ref[slot * TILE : (slot + 2) * TILE, LANES:])
        out_t = out_t.astype(jnp.bfloat16).astype(jnp.float32)
        dots = jnp.sum(out_t * grad.astype(jnp.float32).T, axis=0, keepdims=True)
        outs.append((out_t, dots))
    for index, ((query, grad, listed), (score_ref, prob_ref, pair_ref)) in enumerate(zip(jobs, work)):
        out_t, dots = outs[index]
        for start, size in spans:
            rows = slice(start, start + size)
            slope = score_ref[rows] * (prob_ref[rows] - dots)
            pair_ref[rows, :LANES] = slope.astype(jnp.bfloat16)
        terms = nn(pair_ref[...], results[index][0])
        for tile, (start, size) in zip(listed, spans):
            both_sum[tile] += terms[start : start + size]
        pool_key_sum[...] += terms[fine:, :LANES]
        pool_value_sum[...] += terms[fine:, LANES:]
        query_t = contract(coarse_key, pair_ref[fine:, :LANES], 0, 0)
        for slot in range(0, SEL, 2):
            keys_t = jnp.concatenate([key_t[tile] for tile in listed[slot : slot + 2]], axis=1)
            query_t = query_t + nn(keys_t, pair_ref[slot * TILE : (slot + 2) * TILE, :LANES])
        outs[index] = (
            out_t.T.astype(jnp.bfloat16),
            (query_t.T * scaling).astype(jnp.bfloat16),
        )
    return outs


def finish(tile, scratch):
    scaling = HEAD_DIM ** (-0.5)
    both_sum, pool_key_sum, pool_value_sum = scratch
    per_tile = TILE // POOL
    coarse_key = pool_key_sum[pl.ds(tile * per_tile, per_tile), :] * scaling
    coarse_value = pool_value_sum[pl.ds(tile * per_tile, per_tile), :]

    def whole(fine, coarse):
        return jnp.concatenate(
            [
                fine[part * POOL : (part + 1) * POOL] + coarse[part : part + 1] * (1.0 / POOL)
                for part in range(per_tile)
            ],
            axis=0,
        )

    return (
        whole(both_sum[tile, :, :LANES] * scaling, coarse_key),
        whole(both_sum[tile, :, LANES:], coarse_value),
        coarse_key,
        coarse_value,
    )


def job_count(queries):
    return next(count for count in JOBS if queries % count == 0)


def head_scratch(tiles, jobs):
    comp = tiles * (TILE // POOL)
    keys = SEL * TILE + comp
    return [
        pltpu.VMEM((tiles, TILE, 2 * LANES), jnp.bfloat16),
        pltpu.VMEM((comp, LANES), jnp.float32),
        pltpu.VMEM((comp, LANES), jnp.float32),
        pltpu.VMEM((tiles, LANES, TILE), jnp.bfloat16),
        pltpu.VMEM((tiles, LANES, TILE), jnp.bfloat16),
        pltpu.VMEM((tiles, TILE, 2 * LANES), jnp.float32),
        pltpu.VMEM((comp, LANES), jnp.float32),
        pltpu.VMEM((comp, LANES), jnp.float32),
    ] + jobs * [
        pltpu.VMEM((keys, LANES), jnp.float32),
        pltpu.VMEM((keys, LANES), jnp.float32),
        pltpu.VMEM((keys, 2 * LANES), jnp.bfloat16),
    ]


def split_scratch(scratch):
    totals, work = scratch[:8], scratch[8:]
    return totals, [work[first : first + 3] for first in range(0, len(work), 3)]


def head_cost(queries, keys, moved):
    return pl.CostEstimate(
        flops=12 * queries * keys * LANES,
        transcendentals=queries * keys,
        bytes_accessed=moved,
    )


def every_tile(count, stride, place_ref, sel_ref, query_ref, out_ref, totals, work):
    place = place_ref[0]
    group = len(work)

    def some(first, carry):
        jobs = []
        for job in range(group):
            piece = first * group + job
            tile = lax.bitwise_xor(place, piece * stride)
            listed = [lax.bitwise_xor(sel_ref[tile, slot], place) for slot in range(SEL)]
            jobs.append((query_ref[piece, :, :LANES], query_ref[piece, :, LANES:], listed))
        for job, (rows, slopes) in enumerate(some_tiles(jobs, totals, work)):
            out_ref[first * group + job, :TILE, :] = rows
            out_ref[first * group + job, TILE : 2 * TILE, :] = slopes
        return carry

    lax.fori_loop(0, count // group, some, 0)


def whole_head(tiles, place_ref, sel_ref, *refs):
    pieces, outs = refs[:tiles][::-1], refs[tiles : 2 * tiles]
    query_ref, out_ref = refs[2 * tiles : 2 * tiles + 2]
    totals, work = split_scratch(refs[2 * tiles + 2 :])
    for step, piece in enumerate(pieces):
        query_ref[step, :, :LANES] = piece[:TILE, :]
        totals[0][step, :, :LANES] = piece[TILE : 2 * TILE, :]
        totals[0][step, :, LANES:] = piece[2 * TILE : 3 * TILE, :]
        query_ref[step, :, LANES:] = piece[3 * TILE :, :]
    prepare(totals)
    every_tile(tiles, 1, place_ref, sel_ref, query_ref, out_ref, totals, work)
    for step, out in enumerate(outs):
        key, value, coarse_key, coarse_value = finish(step, totals[5:])
        out[: 2 * TILE, :] = out_ref[step]
        out[2 * TILE : 3 * TILE, :] = key.astype(jnp.bfloat16)
        out[3 * TILE : 4 * TILE, :] = value.astype(jnp.bfloat16)
        out[4 * TILE :, :] = tail_rows(coarse_key, coarse_value)


def shared_head(span, planes, place_ref, sel_ref, *refs):
    owns, refs = refs[:planes], refs[planes:]
    pieces, refs = refs[: span - 1], refs[span - 1 :]
    out_ref, keep_ref, send_ref, query_ref = refs[:4]
    totals, work = split_scratch(refs[4:])
    for plane, own in enumerate(owns):
        query_ref[plane, :, :LANES] = own[:TILE, :]
        query_ref[plane, :, LANES:] = own[3 * TILE :, :]
        totals[0][plane * span, :, :LANES] = own[TILE : 2 * TILE, :]
        totals[0][plane * span, :, LANES:] = own[2 * TILE : 3 * TILE, :]
        for step in range(1, span):
            piece = pieces[step - 1]
            totals[0][plane * span + step, :, :LANES] = piece[plane, :TILE, :]
            totals[0][plane * span + step, :, LANES:] = piece[plane, TILE:, :]
    prepare(totals)
    every_tile(planes, span, place_ref, sel_ref, query_ref, out_ref, totals, work)
    for step in range(span):

        def last(plane, carry, step=step):
            terms = finish(plane * span + step, totals[5:])
            if step % 2 == 0:
                keep_terms(keep_ref, step // 2, plane, *terms)
            else:
                send_terms(send_ref, step // 2, plane, *terms)
            return carry

        lax.fori_loop(0, planes, last, 0)


def keep_terms(ref, index, plane, key, value, coarse_key, coarse_value):
    rows = [coarse_key, coarse_value]
    filler = 8 - 2 * (TILE // POOL)
    if filler:
        rows.append(jnp.zeros((filler, LANES), jnp.float32))
    ref[index, plane, :TILE, :] = key
    ref[index, plane, TILE : 2 * TILE, :] = value
    ref[index, plane, 2 * TILE :, :] = jnp.concatenate(rows, axis=0)


def send_terms(ref, index, plane, key, value, coarse_key, coarse_value):
    ref[index, plane, :TILE, :] = key.astype(jnp.bfloat16)
    ref[index, plane, TILE : 2 * TILE, :] = value.astype(jnp.bfloat16)
    ref[index, plane, 2 * TILE :, :] = tail_rows(coarse_key, coarse_value)


def add_terms(keep_ref, piece_ref, index, plane):
    per_tile = TILE // POOL
    fine = keep_ref[index, plane, : 2 * TILE, :]
    fine = fine + piece_ref[index, plane, : 2 * TILE, :].astype(jnp.float32)
    coarse = keep_ref[index, plane, 2 * TILE : 2 * TILE + 2 * per_tile, :]
    coarse = coarse + join_tail(piece_ref[index, plane, 2 * TILE :, :])
    return fine[:TILE], fine[TILE:], coarse[:per_tile], coarse[per_tile:]


def fold_terms(count, planes, keep_ref, piece_ref, next_ref, send_ref):
    for index in range(count):
        for plane in range(planes):
            terms = add_terms(keep_ref, piece_ref, index, plane)
            if index % 2 == 0:
                keep_terms(next_ref, index // 2, plane, *terms)
            else:
                send_terms(send_ref, index // 2, plane, *terms)


def last_terms(rows_ref, keep_ref, piece_ref, *outs):
    for plane, out in enumerate(outs):
        key, value, coarse_key, coarse_value = add_terms(keep_ref, piece_ref, 0, plane)
        out[: 2 * TILE, :] = rows_ref[plane]
        out[2 * TILE : 3 * TILE, :] = key.astype(jnp.bfloat16)
        out[3 * TILE : 4 * TILE, :] = value.astype(jnp.bfloat16)
        out[4 * TILE :, :] = tail_rows(coarse_key, coarse_value)


def unpack_body(heads, span, place_ref, *refs):
    pieces, (a_ref, q_ref, k_ref, v_ref, pk_ref, pv_ref) = refs[:-6], refs[-6:]
    pieces = pieces[:heads][::-1] + pieces[heads:][::-1]
    per_tile = TILE // POOL
    place = place_ref[0]
    for step, ref in enumerate(pieces):
        if step < heads:
            head = lax.bitwise_xor(place, step)
        else:
            head = heads + lax.bitwise_xor(place // span, step - heads)
        columns = lane_block(head)
        for index, out in enumerate((a_ref, q_ref, k_ref, v_ref)):
            out[:, columns] = ref[index * TILE : (index + 1) * TILE, :]
        coarse = join_tail(ref[4 * TILE :, :])
        pk_ref[:, columns] = coarse[:per_tile]
        pv_ref[:, columns] = coarse[per_tile:]


def head_shards(query_rows, key_rows, value_rows, out_grad, selected):
    devices = lax.axis_size("ctx")
    height, columns = query_rows.shape
    planes = HEADS - devices
    span = devices // planes
    arrays = (query_rows, key_rows, value_rows, out_grad)
    place = jnp.reshape(lax.axis_index("ctx"), (1,))

    def shift(block, step):
        return lax.ppermute(block, "ctx", [(i, i ^ step) for i in range(devices)])

    def spread(pieces, stride):
        moved = [pieces[0]]
        for step in range(1, len(pieces)):
            moved.append(shift(pieces[step], step * stride))
        return moved

    def shape(*dims, dtype=jnp.bfloat16):
        return jax.ShapeDtypeStruct(dims, dtype)

    block = 4 * TILE + tail_height()
    part = 2 * TILE + tail_height()
    keys = SEL * TILE + devices * (TILE // POOL)
    owns = spread(pack(arrays, place // span, devices, planes), span)
    mains = spread(pack(arrays, place, 0, devices), 1)
    own_kv = jnp.stack([own[TILE : 3 * TILE] for own in owns])
    pieces = {0: own_kv}
    hops = [1 << bit for bit in reversed(range(span.bit_length() - 1))]
    for hop in hops:
        held = sorted(pieces)
        for step in held:
            pieces[step ^ hop] = shift(pieces[step], hop)
    pieces = [pieces[step] for step in range(1, span)]
    half = span // 2
    rows, keep, send = pl.pallas_call(
        functools.partial(shared_head, span, planes),
        in_specs=[SMEM, SMEM] + [VMEM] * (planes + span - 1),
        out_specs=[VMEM] * 3,
        out_shape=[
            shape(planes, 2 * TILE, LANES),
            shape(half, planes, 2 * TILE + 8, LANES, dtype=jnp.float32),
            shape(half, planes, part, LANES),
        ],
        scratch_shapes=[pltpu.VMEM((planes, TILE, 2 * LANES), jnp.bfloat16)]
        + head_scratch(devices, job_count(planes)),
        compiler_params=BIG,
        cost_estimate=head_cost(planes * TILE, keys, 16 * devices * TILE * LANES),
        name="shared_head",
    )(place, selected, *owns, *pieces)
    hop = 1
    while half > 1:
        got = shift(send, hop)
        keep, send = pl.pallas_call(
            functools.partial(fold_terms, half, planes),
            in_specs=[VMEM] * 2,
            out_specs=[VMEM] * 2,
            out_shape=[
                shape(half // 2, planes, 2 * TILE + 8, LANES, dtype=jnp.float32),
                shape(half // 2, planes, part, LANES),
            ],
            compiler_params=BIG,
            name="fold_terms",
        )(keep, got)
        half, hop = half // 2, hop * 2
    got = shift(send, hop)
    rests = pl.pallas_call(
        last_terms,
        in_specs=[VMEM] * 3,
        out_specs=[VMEM] * planes,
        out_shape=[shape(block, LANES)] * planes,
        compiler_params=BIG,
        name="last_terms",
    )(rows, keep, got)
    rests = spread(rests, span)
    dones = pl.pallas_call(
        functools.partial(whole_head, devices),
        in_specs=[SMEM, SMEM] + [VMEM] * devices,
        out_specs=[VMEM] * devices,
        out_shape=[shape(block, LANES)] * devices,
        scratch_shapes=[
            pltpu.VMEM((devices, TILE, 2 * LANES), jnp.bfloat16),
            pltpu.VMEM((devices, 2 * TILE, LANES), jnp.bfloat16),
        ]
        + head_scratch(devices, job_count(devices)),
        compiler_params=BIG,
        cost_estimate=head_cost(devices * TILE, keys, 16 * devices * TILE * LANES),
        name="whole_head",
    )(place, selected, *mains[::-1])
    dones = spread(dones, 1)
    wide = shape(height, columns)
    thin = shape(height // POOL, columns, dtype=jnp.float32)
    return pl.pallas_call(
        functools.partial(unpack_body, devices, span),
        in_specs=[SMEM] + [VMEM] * HEADS,
        out_specs=[VMEM] * 6,
        out_shape=[wide, wide, wide, wide, thin, thin],
        compiler_params=BIG,
        name="unpack",
    )(place, *dones[::-1], *rests[::-1])


def shards(query_rows, key_rows, value_rows, out_grad, selected):
    devices = lax.axis_size("ctx")
    planes = HEADS - devices
    tiles_here = query_rows.shape[0] // TILE
    if planes > 0 and devices % planes == 0 and tiles_here == 1:
        span = devices // planes
        if span & (span - 1) == 0:
            return head_shards(query_rows, key_rows, value_rows, out_grad, selected)
    return listed_shards(query_rows, key_rows, value_rows, out_grad, selected)


def solution(mesh):
    in_specs = (
        P(("groups", "ctx"), None),
        P(("groups", "ctx"), None),
        P(("groups", "ctx"), None),
        P(("groups", "ctx"), None),
        P("groups", None),
    )
    out_specs = (
        P(("groups", "ctx"), None),
        P(("groups", "ctx"), None),
        P(("groups", "ctx"), None),
        P(("groups", "ctx"), None),
        P(("groups", "ctx"), None),
        P(("groups", "ctx"), None),
    )
    return jax.shard_map(
        shards, mesh=mesh, in_specs=in_specs, out_specs=out_specs, check_vma=False
    )
```

```python
import functools

import jax
import jax.numpy as jnp
from jax import lax
from jax.experimental import pallas as pl
from jax.experimental.pallas import tpu as pltpu
from jax.sharding import PartitionSpec as P


HEADS = 20
HEAD_DIM = 128
TILE = 128
POOL = 64
SEL = 8


def pooled(rows):
    return jnp.mean(rows.astype(jnp.float32).reshape(-1, POOL, rows.shape[1]), axis=1).astype(
        jnp.bfloat16
    )


def contract(left, right, left_dim, right_dim):
    return lax.dot_general(
        left, right, (((left_dim,), (right_dim,)), ((), ())), preferred_element_type=jnp.float32
    )


def attend(queries, grads_out, keys_all, values_all):
    scaling = HEAD_DIM ** (-0.5)
    out_parts, query_parts, key_parts, value_parts = ([], [], [], [])
    for head in range(HEADS):
        lower = head * HEAD_DIM
        upper = lower + HEAD_DIM
        head_query = queries[:, lower:upper]
        head_grad = grads_out[:, lower:upper]
        head_key = keys_all[:, lower:upper]
        head_value = values_all[:, lower:upper]
        scores = contract(head_query, head_key, 1, 1) * scaling
        summit = jnp.max(scores, axis=-1, keepdims=True)
        raised = jnp.exp(scores - summit)
        weights = raised / jnp.sum(raised, axis=-1, keepdims=True)
        rounded = weights.astype(jnp.bfloat16)
        out_rows = jnp.dot(rounded, head_value, preferred_element_type=jnp.float32).astype(
            jnp.bfloat16
        )
        row_dots = jnp.sum(
            head_grad.astype(jnp.float32) * out_rows.astype(jnp.float32), axis=-1, keepdims=True
        )
        prob_grad = contract(head_grad, head_value, 1, 1)
        score_grad = (weights * (prob_grad - row_dots)).astype(jnp.bfloat16)
        query_grad = jnp.dot(score_grad, head_key, preferred_element_type=jnp.float32) * scaling
        key_terms = contract(score_grad, head_query, 0, 0) * scaling
        value_terms = contract(rounded, head_grad, 0, 0)
        out_parts.append(out_rows)
        query_parts.append(query_grad.astype(jnp.bfloat16))
        key_parts.append(key_terms)
        value_parts.append(value_terms)
    return (
        jnp.concatenate(out_parts, axis=1),
        jnp.concatenate(query_parts, axis=1),
        jnp.concatenate(key_parts, axis=1),
        jnp.concatenate(value_parts, axis=1),
    )


def package(tiles_in, pooled_in, devices, spread):
    tiles_here, tile_len, columns = tiles_in.shape
    per_tile = tile_len // POOL
    split_rows = tiles_in.reshape(tiles_here, devices, spread, columns)
    copies = jnp.broadcast_to(
        pooled_in.reshape(tiles_here, 1, per_tile, columns),
        (tiles_here, devices, per_tile, columns),
    )
    return jnp.concatenate([split_rows, copies], axis=2).reshape(
        tiles_here, devices * (spread + per_tile), columns
    )


def listed_shards(query_rows, key_rows, value_rows, out_grad, selected):
    height, columns = query_rows.shape
    devices = lax.axis_size("ctx")
    tiles_here = height // TILE
    spread = TILE // devices
    own_keys = pooled(key_rows)
    own_values = pooled(value_rows)
    key_tiles = key_rows.reshape(tiles_here, TILE, columns)
    value_tiles = value_rows.reshape(tiles_here, TILE, columns)
    joined_keys, joined_values = (
        lax.all_to_all(
            package(key_tiles, own_keys, devices, spread),
            "ctx",
            split_axis=1,
            concat_axis=0,
            tiled=True,
        ),
        lax.all_to_all(
            package(value_tiles, own_values, devices, spread),
            "ctx",
            split_axis=1,
            concat_axis=0,
            tiled=True,
        ),
    )
    held_keys = joined_keys[:, :spread]
    held_values = joined_values[:, :spread]
    pool_keys = joined_keys[:, spread:].reshape(-1, columns)
    pool_values = joined_values[:, spread:].reshape(-1, columns)
    comp_count = pool_keys.shape[0]
    got_keys, got_values = (
        lax.all_to_all(held_keys[selected], "ctx", split_axis=0, concat_axis=2, tiled=True),
        lax.all_to_all(held_values[selected], "ctx", split_axis=0, concat_axis=2, tiled=True),
    )
    fine_keys = got_keys.reshape(tiles_here, SEL * TILE, columns)
    fine_values = got_values.reshape(tiles_here, SEL * TILE, columns)
    out_tiles, query_tiles, key_listed, value_listed = ([], [], [], [])
    keys_all = jnp.concatenate([pool_keys, fine_keys[0]], axis=0)
    values_all = jnp.concatenate([pool_values, fine_values[0]], axis=0)
    out_rows, query_grad, key_terms, value_terms = attend(
        query_rows, out_grad, keys_all, values_all
    )
    out_tiles.append(out_rows)
    query_tiles.append(query_grad)
    coarse_keys = key_terms[:comp_count]
    coarse_values = value_terms[:comp_count]
    key_listed.append(key_terms[comp_count:].astype(jnp.bfloat16))
    value_listed.append(value_terms[comp_count:].astype(jnp.bfloat16))
    own_coarse_keys, own_coarse_values = (
        lax.psum_scatter(coarse_keys, "ctx", scatter_dimension=0, tiled=True),
        lax.psum_scatter(coarse_values, "ctx", scatter_dimension=0, tiled=True),
    )
    listed_keys = jnp.stack(key_listed).reshape(tiles_here * SEL, devices, spread, columns)
    listed_values = jnp.stack(value_listed).reshape(tiles_here * SEL, devices, spread, columns)
    back_keys, back_values = (
        lax.all_to_all(listed_keys, "ctx", split_axis=1, concat_axis=0, tiled=True),
        lax.all_to_all(listed_values, "ctx", split_axis=1, concat_axis=0, tiled=True),
    )
    tile_ids = jnp.arange(selected.shape[0], dtype=jnp.int32)[:, None]
    member = (selected.reshape(1, -1) == tile_ids).astype(jnp.bfloat16)
    entries = member.shape[1]
    sum_keys = jnp.dot(
        member, back_keys.reshape(entries, spread * columns), preferred_element_type=jnp.float32
    )
    sum_values = jnp.dot(
        member, back_values.reshape(entries, spread * columns), preferred_element_type=jnp.float32
    )
    held_key_grad = sum_keys.astype(jnp.bfloat16).reshape(devices, tiles_here, spread, columns)
    held_value_grad = sum_values.astype(jnp.bfloat16).reshape(devices, tiles_here, spread, columns)
    owned_keys, owned_values = (
        lax.all_to_all(held_key_grad, "ctx", split_axis=0, concat_axis=2, tiled=True),
        lax.all_to_all(held_value_grad, "ctx", split_axis=0, concat_axis=2, tiled=True),
    )
    grad_key = (
        owned_keys.reshape(height, columns).astype(jnp.float32)
        + jnp.repeat(own_coarse_keys, POOL, axis=0) / POOL
    ).astype(jnp.bfloat16)
    grad_value = (
        owned_values.reshape(height, columns).astype(jnp.float32)
        + jnp.repeat(own_coarse_values, POOL, axis=0) / POOL
    ).astype(jnp.bfloat16)
    attended = out_tiles[0]
    grad_query = query_tiles[0]
    return (attended, grad_query, grad_key, grad_value, own_coarse_keys, own_coarse_values)


LANES = 128
JOBS = (8, 4, 2, 1)
SPLITS = 2
VMEM = pl.BlockSpec(memory_space=pltpu.VMEM)
SMEM = pl.BlockSpec(memory_space=pltpu.SMEM)
BIG = pltpu.CompilerParams(vmem_limit_bytes=32 * 1024 * 1024)


def nt(left, right):
    return contract(left, right, 1, 1)


def nn(left, right):
    return contract(left, right, 1, 0)


def split_rows(total):
    parts = []
    for _ in range(SPLITS):
        part = total.astype(jnp.bfloat16)
        parts.append(part.astype(jnp.float32))
        total = total - parts[-1]
    return parts


def tail_rows(coarse_key, coarse_value):
    per_tile = TILE // POOL
    parts = split_rows(jnp.concatenate([coarse_key, coarse_value], axis=0))
    used = SPLITS * 2 * per_tile
    if used < tail_height():
        parts.append(jnp.zeros((tail_height() - used, LANES), jnp.float32))
    return jnp.concatenate(parts, axis=0).astype(jnp.bfloat16)


def tail_height():
    used = SPLITS * 2 * (TILE // POOL)
    return -(-used // 8) * 8


def join_tail(tail):
    pair = 2 * (TILE // POOL)
    rows = tail.astype(jnp.float32)
    total = rows[:pair]
    for part in range(1, SPLITS):
        total = total + rows[part * pair : (part + 1) * pair]
    return total


def lane_block(index):
    return pl.ds(pl.multiple_of(index * LANES, LANES), LANES)


def pack_body(first, place_ref, q_ref, k_ref, v_ref, g_ref, *out_refs):
    for step, out_ref in enumerate(out_refs):
        columns = lane_block(first + lax.bitwise_xor(place_ref[0], step))
        for index, ref in enumerate((q_ref, k_ref, v_ref, g_ref)):
            out_ref[index * TILE : (index + 1) * TILE, :] = ref[:, columns]


def pack(arrays, place, first, count):
    width = arrays[0].shape[1]
    if first % count == 0:
        spec = pl.BlockSpec((TILE, count * LANES), lambda i, _: (0, first // count))
        start = 0
    else:
        spec = pl.BlockSpec((TILE, width), lambda i, _: (0, 0))
        start = first
    out = pl.BlockSpec((4 * TILE, LANES), lambda i, _: (0, 0))
    return pl.pallas_call(
        functools.partial(pack_body, start),
        grid_spec=pltpu.PrefetchScalarGridSpec(
            num_scalar_prefetch=1, grid=(1,), in_specs=[spec] * 4, out_specs=[out] * count
        ),
        out_shape=[jax.ShapeDtypeStruct((4 * TILE, LANES), jnp.bfloat16)] * count,
        cost_estimate=pl.CostEstimate(
            flops=0, transcendentals=0, bytes_accessed=16 * count * TILE * LANES
        ),
        name="pack",
    )(place, *arrays)


def prepare(scratch, unroll=1):
    rows_ref, pool_key, pool_value, key_t, value_t, both_sum, pool_key_sum, pool_value_sum = scratch
    per_tile = TILE // POOL

    def one(tile, carry):
        for place, pool_ref, flip_ref in ((0, pool_key, key_t), (1, pool_value, value_t)):
            rows = rows_ref[tile, :, place * LANES : (place + 1) * LANES].astype(jnp.float32)
            means = [
                jnp.mean(rows[part * POOL : (part + 1) * POOL], axis=0, keepdims=True)
                for part in range(per_tile)
            ]
            pool_ref[pl.ds(tile * per_tile, per_tile), :] = jnp.concatenate(means, axis=0)
            flip_ref[tile] = rows.T.astype(jnp.bfloat16)
        both_sum[tile] = jnp.zeros((TILE, 2 * LANES), jnp.float32)
        return carry

    lax.fori_loop(0, rows_ref.shape[0], one, 0, unroll=unroll)
    pool_key_sum[...] = jnp.zeros_like(pool_key_sum)
    pool_value_sum[...] = jnp.zeros_like(pool_value_sum)


def wide_pair(left, right):
    zeros = jnp.zeros_like(left)
    return jnp.concatenate(
        [jnp.concatenate([left, zeros], axis=1), jnp.concatenate([zeros, right], axis=1)], axis=0
    )


def some_tiles(jobs, scratch, work):
    rows_ref, pool_key, pool_value, key_t, value_t, both_sum, pool_key_sum, pool_value_sum = scratch
    scaling = HEAD_DIM ** (-0.5)
    base2 = scaling * 1.4426950408889634
    comp = pool_key.shape[0]
    coarse_key = pool_key[...].astype(jnp.bfloat16)
    coarse_value = pool_value[...].astype(jnp.bfloat16)
    coarse = jnp.concatenate([coarse_key, coarse_value], axis=1)
    fine = SEL * TILE
    spans = [(slot * TILE, TILE) for slot in range(SEL)] + [(fine, comp)]
    results = []
    for (query, grad, listed), (score_ref, prob_ref, pair_ref) in zip(jobs, work):
        pair = wide_pair(query, grad)
        rows = [rows_ref[tile] for tile in listed]
        both = nt(jnp.concatenate(rows + [coarse], axis=0), pair)
        score_ref[...] = both[:, :LANES]
        prob_ref[...] = both[:, LANES:]
        top = jnp.max(both[:, :LANES], axis=0, keepdims=True)
        results.append((pair, top))
    for index, (_, (score_ref, prob_ref, pair_ref)) in enumerate(zip(jobs, work)):
        pair, top = results[index]
        total = jnp.zeros((8, LANES), jnp.float32)
        for start, size in spans:
            raised = jnp.exp2((score_ref[start : start + size] - top) * base2)
            score_ref[start : start + size] = raised
            total = total + jnp.sum(raised.reshape(size // 8, 8, LANES), axis=0)
        inverse = 1.0 / jnp.sum(total, axis=0, keepdims=True)
        results[index] = (pair, inverse)
    outs = []
    for index, ((query, grad, listed), (score_ref, prob_ref, pair_ref)) in enumerate(zip(jobs, work)):
        pair, inverse = results[index]
        for start, size in spans:
            weight = score_ref[start : start + size] * inverse
            pair_ref[start : start + size, LANES:] = weight.astype(jnp.bfloat16)
            score_ref[start : start + size] = weight
        out_t = contract(coarse_value, pair_ref[fine:, LANES:], 0, 0)
        for slot in range(0, SEL, 2):
            values_t = jnp.concatenate([value_t[tile] for tile in listed[slot : slot + 2]], axis=1)
            out_t = out_t + nn(values_t, pair_ref[slot * TILE : (slot + 2) * TILE, LANES:])
        out_t = out_t.astype(jnp.bfloat16).astype(jnp.float32)
        dots = jnp.sum(out_t * grad.astype(jnp.float32).T, axis=0, keepdims=True)
        outs.append((out_t, dots))
    for index, ((query, grad, listed), (score_ref, prob_ref, pair_ref)) in enumerate(zip(jobs, work)):
        out_t, dots = outs[index]
        for start, size in spans:
            rows = slice(start, start + size)
            slope = score_ref[rows] * (prob_ref[rows] - dots)
            pair_ref[rows, :LANES] = slope.astype(jnp.bfloat16)
        terms = nn(pair_ref[...], results[index][0])
        for tile, (start, size) in zip(listed, spans):
            both_sum[tile] += terms[start : start + size]
        pool_key_sum[...] += terms[fine:, :LANES]
        pool_value_sum[...] += terms[fine:, LANES:]
        query_t = contract(coarse_key, pair_ref[fine:, :LANES], 0, 0)
        for slot in range(0, SEL, 2):
            keys_t = jnp.concatenate([key_t[tile] for tile in listed[slot : slot + 2]], axis=1)
            query_t = query_t + nn(keys_t, pair_ref[slot * TILE : (slot + 2) * TILE, :LANES])
        outs[index] = (
            out_t.T.astype(jnp.bfloat16),
            (query_t.T * scaling).astype(jnp.bfloat16),
        )
    return outs


def finish(tile, scratch):
    scaling = HEAD_DIM ** (-0.5)
    both_sum, pool_key_sum, pool_value_sum = scratch
    per_tile = TILE // POOL
    coarse_key = pool_key_sum[pl.ds(tile * per_tile, per_tile), :] * scaling
    coarse_value = pool_value_sum[pl.ds(tile * per_tile, per_tile), :]

    def whole(fine, coarse):
        return jnp.concatenate(
            [
                fine[part * POOL : (part + 1) * POOL] + coarse[part : part + 1] * (1.0 / POOL)
                for part in range(per_tile)
            ],
            axis=0,
        )

    return (
        whole(both_sum[tile, :, :LANES] * scaling, coarse_key),
        whole(both_sum[tile, :, LANES:], coarse_value),
        coarse_key,
        coarse_value,
    )


def job_count(queries):
    return next(count for count in JOBS if queries % count == 0)


def head_scratch(tiles, jobs):
    comp = tiles * (TILE // POOL)
    keys = SEL * TILE + comp
    return [
        pltpu.VMEM((tiles, TILE, 2 * LANES), jnp.bfloat16),
        pltpu.VMEM((comp, LANES), jnp.float32),
        pltpu.VMEM((comp, LANES), jnp.float32),
        pltpu.VMEM((tiles, LANES, TILE), jnp.bfloat16),
        pltpu.VMEM((tiles, LANES, TILE), jnp.bfloat16),
        pltpu.VMEM((tiles, TILE, 2 * LANES), jnp.float32),
        pltpu.VMEM((comp, LANES), jnp.float32),
        pltpu.VMEM((comp, LANES), jnp.float32),
    ] + jobs * [
        pltpu.VMEM((keys, LANES), jnp.float32),
        pltpu.VMEM((keys, LANES), jnp.float32),
        pltpu.VMEM((keys, 2 * LANES), jnp.bfloat16),
    ]


def split_scratch(scratch):
    totals, work = scratch[:8], scratch[8:]
    return totals, [work[first : first + 3] for first in range(0, len(work), 3)]


def head_cost(queries, keys, moved):
    return pl.CostEstimate(
        flops=12 * queries * keys * LANES,
        transcendentals=queries * keys,
        bytes_accessed=moved,
    )


def every_tile(count, stride, place_ref, sel_ref, query_ref, out_ref, totals, work):
    place = place_ref[0]
    group = len(work)

    def some(first, carry):
        jobs = []
        for job in range(group):
            piece = first * group + job
            tile = lax.bitwise_xor(place, piece * stride)
            listed = [lax.bitwise_xor(sel_ref[tile, slot], place) for slot in range(SEL)]
            jobs.append((query_ref[piece, :, :LANES], query_ref[piece, :, LANES:], listed))
        for job, (rows, slopes) in enumerate(some_tiles(jobs, totals, work)):
            out_ref[first * group + job, :TILE, :] = rows
            out_ref[first * group + job, TILE : 2 * TILE, :] = slopes
        return carry

    lax.fori_loop(0, count // group, some, 0)


def whole_head(tiles, place_ref, sel_ref, *refs):
    pieces, outs = refs[:tiles][::-1], refs[tiles : 2 * tiles]
    query_ref, out_ref = refs[2 * tiles : 2 * tiles + 2]
    totals, work = split_scratch(refs[2 * tiles + 2 :])
    for step, piece in enumerate(pieces):
        query_ref[step, :, :LANES] = piece[:TILE, :]
        totals[0][step, :, :LANES] = piece[TILE : 2 * TILE, :]
        totals[0][step, :, LANES:] = piece[2 * TILE : 3 * TILE, :]
        query_ref[step, :, LANES:] = piece[3 * TILE :, :]
    prepare(totals, unroll=8)
    every_tile(tiles, 1, place_ref, sel_ref, query_ref, out_ref, totals, work)
    for step, out in enumerate(outs):
        key, value, coarse_key, coarse_value = finish(step, totals[5:])
        out[: 2 * TILE, :] = out_ref[step]
        out[2 * TILE : 3 * TILE, :] = key.astype(jnp.bfloat16)
        out[3 * TILE : 4 * TILE, :] = value.astype(jnp.bfloat16)
        out[4 * TILE :, :] = tail_rows(coarse_key, coarse_value)


def shared_head(span, planes, place_ref, sel_ref, *refs):
    owns, refs = refs[:planes], refs[planes:]
    pieces, refs = refs[: span - 1], refs[span - 1 :]
    out_ref, keep_ref, send_ref, query_ref = refs[:4]
    totals, work = split_scratch(refs[4:])
    for plane, own in enumerate(owns):
        query_ref[plane, :, :LANES] = own[:TILE, :]
        query_ref[plane, :, LANES:] = own[3 * TILE :, :]
        totals[0][plane * span, :, :LANES] = own[TILE : 2 * TILE, :]
        totals[0][plane * span, :, LANES:] = own[2 * TILE : 3 * TILE, :]
        for step in range(1, span):
            piece = pieces[step - 1]
            totals[0][plane * span + step, :, :LANES] = piece[plane, :TILE, :]
            totals[0][plane * span + step, :, LANES:] = piece[plane, TILE:, :]
    prepare(totals)
    every_tile(planes, span, place_ref, sel_ref, query_ref, out_ref, totals, work)
    for step in range(span):

        def last(plane, carry, step=step):
            terms = finish(plane * span + step, totals[5:])
            if step % 2 == 0:
                keep_terms(keep_ref, step // 2, plane, *terms)
            else:
                send_terms(send_ref, step // 2, plane, *terms)
            return carry

        lax.fori_loop(0, planes, last, 0)


def keep_terms(ref, index, plane, key, value, coarse_key, coarse_value):
    rows = [coarse_key, coarse_value]
    filler = 8 - 2 * (TILE // POOL)
    if filler:
        rows.append(jnp.zeros((filler, LANES), jnp.float32))
    ref[index, plane, :TILE, :] = key
    ref[index, plane, TILE : 2 * TILE, :] = value
    ref[index, plane, 2 * TILE :, :] = jnp.concatenate(rows, axis=0)


def send_terms(ref, index, plane, key, value, coarse_key, coarse_value):
    ref[index, plane, :TILE, :] = key.astype(jnp.bfloat16)
    ref[index, plane, TILE : 2 * TILE, :] = value.astype(jnp.bfloat16)
    ref[index, plane, 2 * TILE :, :] = tail_rows(coarse_key, coarse_value)


def add_terms(keep_ref, piece_ref, index, plane):
    per_tile = TILE // POOL
    fine = keep_ref[index, plane, : 2 * TILE, :]
    fine = fine + piece_ref[index, plane, : 2 * TILE, :].astype(jnp.float32)
    coarse = keep_ref[index, plane, 2 * TILE : 2 * TILE + 2 * per_tile, :]
    coarse = coarse + join_tail(piece_ref[index, plane, 2 * TILE :, :])
    return fine[:TILE], fine[TILE:], coarse[:per_tile], coarse[per_tile:]


def fold_terms(count, planes, keep_ref, piece_ref, next_ref, send_ref):
    for index in range(count):
        for plane in range(planes):
            terms = add_terms(keep_ref, piece_ref, index, plane)
            if index % 2 == 0:
                keep_terms(next_ref, index // 2, plane, *terms)
            else:
                send_terms(send_ref, index // 2, plane, *terms)


def last_terms(rows_ref, keep_ref, piece_ref, *outs):
    for plane, out in enumerate(outs):
        key, value, coarse_key, coarse_value = add_terms(keep_ref, piece_ref, 0, plane)
        out[: 2 * TILE, :] = rows_ref[plane]
        out[2 * TILE : 3 * TILE, :] = key.astype(jnp.bfloat16)
        out[3 * TILE : 4 * TILE, :] = value.astype(jnp.bfloat16)
        out[4 * TILE :, :] = tail_rows(coarse_key, coarse_value)


def head_of(place, step, heads, span):
    if step < heads:
        return lax.bitwise_xor(place, step)
    return heads + lax.bitwise_xor(place // span, step - heads)


def unpack_body(heads, span, steps, place_ref, *refs):
    pieces, refs = refs[: len(steps)], refs[len(steps) :]
    outs, pooled_rows, sem = refs[-7:-3], refs[-3:-1], refs[-1]
    place = place_ref[0]
    per_tile = TILE // POOL
    copies = []
    for row, (step, piece) in enumerate(zip(steps, pieces)):
        columns = lane_block(head_of(place, step, heads, span))
        for index, out in enumerate(outs):
            source = piece.at[index * TILE : (index + 1) * TILE, :]
            copies.append(pltpu.make_async_copy(source, out.at[:, columns], sem.at[row, index]))
            copies[-1].start()
    if len(refs) > 7:
        for old, new in zip(refs[4:6], pooled_rows):
            new[...] = old[...]
    for step, piece in zip(steps, pieces):
        columns = lane_block(head_of(place, step, heads, span))
        coarse = join_tail(piece[4 * TILE :, :])
        for index, out in enumerate(pooled_rows):
            out[:, columns] = coarse[index * per_tile : (index + 1) * per_tile]
    for copy in copies:
        copy.wait()


def unpack(place, pieces, heads, span, wide, thin):
    every = tuple(range(len(pieces)))
    last = every[heads // 2 : heads // 2 + span]
    early = tuple(step for step in every if step not in last)
    anywhere = pl.BlockSpec(memory_space=pl.ANY)
    begun = pl.pallas_call(
        functools.partial(unpack_body, heads, span, early),
        in_specs=[SMEM] + [VMEM] * len(early),
        out_specs=[anywhere] * 4 + [VMEM] * 2,
        out_shape=[wide] * 4 + [thin] * 2,
        scratch_shapes=[pltpu.SemaphoreType.DMA((len(early), 4))],
        compiler_params=BIG,
        name="unpack_early",
    )(place, *[pieces[step] for step in early])
    return pl.pallas_call(
        functools.partial(unpack_body, heads, span, last),
        in_specs=[SMEM] + [VMEM] * len(last) + [anywhere] * 4 + [VMEM] * 2,
        out_specs=[anywhere] * 4 + [VMEM] * 2,
        out_shape=[wide] * 4 + [thin] * 2,
        input_output_aliases={1 + len(last) + index: index for index in range(4)},
        scratch_shapes=[pltpu.SemaphoreType.DMA((len(last), 4))],
        compiler_params=BIG,
        name="unpack_last",
    )(place, *[pieces[step] for step in last], *begun)


def head_shards(query_rows, key_rows, value_rows, out_grad, selected):
    devices = lax.axis_size("ctx")
    height, columns = query_rows.shape
    planes = HEADS - devices
    span = devices // planes
    arrays = (query_rows, key_rows, value_rows, out_grad)
    place = jnp.reshape(lax.axis_index("ctx"), (1,))

    def shift(block, step):
        return lax.ppermute(block, "ctx", [(i, i ^ step) for i in range(devices)])

    def spread(pieces, stride):
        moved = [pieces[0]]
        for step in range(1, len(pieces)):
            moved.append(shift(pieces[step], step * stride))
        return moved

    def shape(*dims, dtype=jnp.bfloat16):
        return jax.ShapeDtypeStruct(dims, dtype)

    block = 4 * TILE + tail_height()
    part = 2 * TILE + tail_height()
    keys = SEL * TILE + devices * (TILE // POOL)
    owns = spread(pack(arrays, place // span, devices, planes), span)
    mains = spread(pack(arrays, place, 0, devices), 1)
    own_kv = jnp.stack([own[TILE : 3 * TILE] for own in owns])
    pieces = {0: own_kv}
    hops = [1 << bit for bit in reversed(range(span.bit_length() - 1))]
    for hop in hops:
        held = sorted(pieces)
        for step in held:
            pieces[step ^ hop] = shift(pieces[step], hop)
    pieces = [pieces[step] for step in range(1, span)]
    half = span // 2
    rows, keep, send = pl.pallas_call(
        functools.partial(shared_head, span, planes),
        in_specs=[SMEM, SMEM] + [VMEM] * (planes + span - 1),
        out_specs=[VMEM] * 3,
        out_shape=[
            shape(planes, 2 * TILE, LANES),
            shape(half, planes, 2 * TILE + 8, LANES, dtype=jnp.float32),
            shape(half, planes, part, LANES),
        ],
        scratch_shapes=[pltpu.VMEM((planes, TILE, 2 * LANES), jnp.bfloat16)]
        + head_scratch(devices, job_count(planes)),
        compiler_params=BIG,
        cost_estimate=head_cost(planes * TILE, keys, 16 * devices * TILE * LANES),
        name="shared_head",
    )(place, selected, *owns, *pieces)
    hop = 1
    while half > 1:
        got = shift(send, hop)
        keep, send = pl.pallas_call(
            functools.partial(fold_terms, half, planes),
            in_specs=[VMEM] * 2,
            out_specs=[VMEM] * 2,
            out_shape=[
                shape(half // 2, planes, 2 * TILE + 8, LANES, dtype=jnp.float32),
                shape(half // 2, planes, part, LANES),
            ],
            compiler_params=BIG,
            name="fold_terms",
        )(keep, got)
        half, hop = half // 2, hop * 2
    got = shift(send, hop)
    rests = pl.pallas_call(
        last_terms,
        in_specs=[VMEM] * 3,
        out_specs=[VMEM] * planes,
        out_shape=[shape(block, LANES)] * planes,
        compiler_params=BIG,
        name="last_terms",
    )(rows, keep, got)
    rests = spread(rests, span)
    dones = pl.pallas_call(
        functools.partial(whole_head, devices),
        in_specs=[SMEM, SMEM] + [VMEM] * devices,
        out_specs=[VMEM] * devices,
        out_shape=[shape(block, LANES)] * devices,
        scratch_shapes=[
            pltpu.VMEM((devices, TILE, 2 * LANES), jnp.bfloat16),
            pltpu.VMEM((devices, 2 * TILE, LANES), jnp.bfloat16),
        ]
        + head_scratch(devices, job_count(devices)),
        compiler_params=BIG,
        cost_estimate=head_cost(devices * TILE, keys, 16 * devices * TILE * LANES),
        name="whole_head",
    )(place, selected, *mains[::-1])
    dones = spread(dones, 1)
    wide = shape(height, columns)
    thin = shape(height // POOL, columns, dtype=jnp.float32)
    return unpack(place, dones + rests, devices, span, wide, thin)


def shards(query_rows, key_rows, value_rows, out_grad, selected):
    devices = lax.axis_size("ctx")
    planes = HEADS - devices
    tiles_here = query_rows.shape[0] // TILE
    if planes > 0 and devices % planes == 0 and tiles_here == 1:
        span = devices // planes
        if span & (span - 1) == 0:
            return head_shards(query_rows, key_rows, value_rows, out_grad, selected)
    return listed_shards(query_rows, key_rows, value_rows, out_grad, selected)


def solution(mesh):
    in_specs = (
        P(("groups", "ctx"), None),
        P(("groups", "ctx"), None),
        P(("groups", "ctx"), None),
        P(("groups", "ctx"), None),
        P("groups", None),
    )
    out_specs = (
        P(("groups", "ctx"), None),
        P(("groups", "ctx"), None),
        P(("groups", "ctx"), None),
        P(("groups", "ctx"), None),
        P(("groups", "ctx"), None),
        P(("groups", "ctx"), None),
    )
    return jax.shard_map(
        shards, mesh=mesh, in_specs=in_specs, out_specs=out_specs, check_vma=False
    )
```
